512 devices in a mesh: dp: 16 (over x_hi, y), ctx: 32 (over z, x_lo, core).
Axes of the slice: x: 4 (x_hi: 2, x_lo: 2; x = x_hi * 2 + x_lo), y: 8, z: 8, core: 2. Of those that a mesh axis runs over, the one named last changes fastest.
Arguments:
- tokens: bfloat16 [16, 4096, 8192], P('dp', 'ctx')
- qkv_weight: bfloat16 [8192, 384], P('dp')
- out_grad: bfloat16 [16, 4096, 128], P('dp', 'ctx'), may hold values from -0.0625 to 0.0625
Outputs:
- attn_out: bfloat16 [16, 4096, 128], P('dp', 'ctx')
- qkv_grad: bfloat16 [8192, 384], P('dp')
The draws below stay inside these ranges and needn't reach their ends.
All inputs are finite; a program needn't handle non-finite values.
Results may differ from the reference program's by a relative error of at most 0.03.
Values may be sent and summed in bfloat16 or wider, within the bound.
No kernel may reach another device: no remote copies, remote signals or barrier semaphores. Data moves between devices by JAX's collectives and lax.ppermute only.
A program may use at most 64 MiB of HBM per device.

```python
import math
import jax
import jax.numpy as jnp
from jax import lax

D = 8192
HD = 128
TOK_DEV = 128
BLK = 64
LEN = 4096
SEQS = 16
N_CTX = 32


def draw_tokens(key, part):
    return jnp.clip(jax.random.normal(jax.random.fold_in(key, 1), (SEQS, LEN, D), jnp.float32), -6.0, 6.0).astype(jnp.bfloat16)


def draw_qkv_weight(key, part):
    base = jnp.clip(jax.random.normal(jax.random.fold_in(key, 4), (D, 3 * HD), jnp.float32), -4.0, 4.0)
    return (base / math.sqrt(D)).astype(jnp.bfloat16)


def block_levels(key, dims, split, smallest, top_value):
    loudness, own = 1.0, jax.random.fold_in(key, 6)
    for dim, blocks in split:
        heights = jnp.exp(jax.random.uniform(jax.random.fold_in(own, dim), (blocks,), jnp.float32, smallest / len(split), top_value / len(split)))
        loudness = loudness * jnp.repeat(heights, dims[dim] // blocks).reshape([-1 if axis == dim else 1 for axis in range(len(dims))])
    return loudness


def scatter_about(stream_key, dims, spread, reach, pieces=(), held_as=jnp.bfloat16):
    factor_of = block_levels(stream_key, dims, pieces, -0.22, 0.18) if pieces else 1.0
    drawn = jax.random.normal(stream_key, dims, jnp.float32) * spread * factor_of
    return jnp.minimum(jnp.maximum(drawn, -reach), reach).astype(held_as)


def setup_inputs(seed: int = 0) -> dict:
    key_list = jax.random.split(jax.random.key(seed), 4)
    return {
        "tokens": draw_tokens(jax.random.fold_in(key_list[3], 71), 0),
        "qkv_weight": draw_qkv_weight(jax.random.fold_in(key_list[3], 71), 0),
        "out_grad": scatter_about(key_list[2], (SEQS, LEN, HD), 0.01, 0.0625, ((0, 16), (1, 32))),
    }


z_weight = 0.001
masked_fill = -1e+30

def stored_positions():
    indices = jnp.arange(LEN, dtype=jnp.int32)
    device_index = indices // TOK_DEV
    inside = indices % TOK_DEV
    block_index = jnp.where(inside < BLK, device_index, 2 * N_CTX - 1 - device_index)
    return (block_index * BLK + inside % BLK).astype(jnp.int32)

def one_sequence(features, weights, cotangent, positions):
    score_scale = 1.0 / math.sqrt(HD)
    qkv = jnp.dot(features, weights, preferred_element_type=jnp.float32).astype(jnp.bfloat16)
    queries = qkv[:, :HD]
    key_rows = qkv[:, HD:2 * HD]
    value_rows = qkv[:, 2 * HD:]
    allowed = positions[None, :] <= positions[:, None]
    scores = jnp.dot(queries, key_rows.T, preferred_element_type=jnp.float32) * score_scale
    scores = jnp.where(allowed, scores, masked_fill)
    row_top = lax.optimization_barrier(jnp.max(scores, axis=1))
    log_total = row_top + jnp.log(lax.optimization_barrier(jnp.sum(jnp.exp(scores - row_top[:, None]), axis=1)))
    probs = jnp.where(allowed, jnp.exp(scores - log_total[:, None]), 0.0)
    probs_low = probs.astype(jnp.bfloat16)
    attn_rows = jnp.dot(probs_low, value_rows, preferred_element_type=jnp.float32).astype(jnp.bfloat16)
    row_delta = lax.optimization_barrier(jnp.sum(cotangent.astype(jnp.float32) * attn_rows.astype(jnp.float32), axis=1))
    dprob = jnp.dot(cotangent, value_rows.T, preferred_element_type=jnp.float32)
    dscore = probs * (dprob - row_delta[:, None] + 2.0 * z_weight * log_total[:, None])
    dscore_low = dscore.astype(jnp.bfloat16)
    grad_query = (jnp.dot(dscore_low, key_rows, preferred_element_type=jnp.float32) * score_scale).astype(jnp.bfloat16)
    grad_key = (jnp.dot(dscore_low.T, queries, preferred_element_type=jnp.float32) * score_scale).astype(jnp.bfloat16)
    grad_value = jnp.dot(probs_low.T, cotangent, preferred_element_type=jnp.float32).astype(jnp.bfloat16)
    grad_rows = jnp.concatenate([grad_query, grad_key, grad_value], axis=1)
    partial_sum = jnp.dot(features.T, grad_rows, preferred_element_type=jnp.float32)
    return (attn_rows, partial_sum)

def reference(tokens, qkv_weight, out_grad):
    positions = stored_positions()

    def sequence_step(running, inputs_pair):
        features, cotangent = inputs_pair
        attn_rows, partial_sum = one_sequence(features, qkv_weight, cotangent, positions)
        return (running + partial_sum, attn_rows)
    running, attn_out = lax.scan(sequence_step, jnp.zeros((D, 3 * HD), jnp.float32), (tokens, out_grad))
    return (attn_out, running.astype(jnp.bfloat16))
```

```python
import math

import jax
import jax.numpy as jnp
from jax import lax
from jax.sharding import Mesh, PartitionSpec as P

z_weight = 0.001
masked_fill = -1e30
low = jnp.bfloat16
ctx_axes = ("z", "xl", "core")


def contract_last(left, right):
    return lax.dot_general(
        left, right, (((1,), (1,)), ((), ())), preferred_element_type=jnp.float32
    )


def contract_first(left, right):
    return lax.dot_general(
        left, right, (((0,), (0,)), ((), ())), preferred_element_type=jnp.float32
    )


def exchange(blocks, axes):
    return lax.all_to_all(blocks, axes, split_axis=0, concat_axis=0, tiled=True)


def spread(block, axes, count):
    return exchange(jnp.broadcast_to(block[None], (count,) + block.shape), axes)


def swap(block, axis):
    return lax.ppermute(block, axis, ((0, 1), (1, 0)))


def gather_rows(block):
    along_z = spread(block, "z", lax.axis_size("z"))
    along_x = jnp.stack([along_z, swap(along_z, "xl")])
    return jnp.stack([along_x, swap(along_x, "core")])


def positions_of(device, inside, half_rows, ctx_count):
    block = jnp.where(inside < half_rows, device, 2 * ctx_count - 1 - device)
    return block * half_rows + inside % half_rows


def on_device(tokens, qkv_weight, out_grad):
    y_count, z_count = lax.axis_size("y"), lax.axis_size("z")
    ctx_count = z_count * 4
    row_count, width = tokens.shape[1], qkv_weight.shape[1]
    shard, head_size = qkv_weight.shape[0], qkv_weight.shape[1] // 3
    half_rows = row_count // 2
    score_scale = 1.0 / math.sqrt(head_size)
    cotangent = out_grad[0]
    x_hi, z_at, x_lo, core = (lax.axis_index(a) for a in ("xh", "z", "xl", "core"))

    other_weight = swap(qkv_weight, "xh")
    first = x_hi == 0
    weight = jnp.concatenate(
        [jnp.where(first, qkv_weight, other_weight), jnp.where(first, other_weight, qkv_weight)]
    )
    split = tokens[0].reshape(row_count, 2, y_count, shard).transpose(2, 0, 1, 3)
    columns = exchange(split.reshape(y_count, row_count, 2 * shard), "y")
    columns = columns.reshape(y_count * row_count, 2 * shard)
    partial_qkv = jnp.dot(columns, weight, preferred_element_type=jnp.float32).astype(low)
    parts = exchange(partial_qkv.reshape(y_count, row_count, width), "y")
    qkv = jnp.sum(parts.astype(jnp.float32), axis=0).astype(low)
    queries, own_keys, own_values = (
        qkv[:, :head_size],
        qkv[:, head_size : 2 * head_size],
        qkv[:, 2 * head_size :],
    )

    gathered = gather_rows(jnp.concatenate([qkv, cotangent], axis=1))
    gathered = gathered.reshape(ctx_count * row_count, 4 * head_size)
    query_all = gathered[:, :head_size]
    key_rows = gathered[:, head_size : 2 * head_size]
    value_rows = gathered[:, 2 * head_size : 3 * head_size]
    cotangent_all = gathered[:, 3 * head_size :]

    own_positions = positions_of(
        z_at * 4 + x_lo * 2 + core, jnp.arange(row_count, dtype=jnp.int32), half_rows, ctx_count
    )
    index = jnp.arange(row_count * ctx_count, dtype=jnp.int32)
    inside, block = index % row_count, index // row_count
    device = (
        (block % z_count) * 4
        + ((block // z_count) % 2 ^ x_lo) * 2
        + (block // (2 * z_count) ^ core)
    )
    all_positions = positions_of(device, inside, half_rows, ctx_count)

    allowed = all_positions[None, :] <= own_positions[:, None]
    scores = jnp.where(allowed, contract_last(queries, key_rows) * score_scale, masked_fill)
    row_top = jnp.max(scores, axis=1)
    log_total = row_top + jnp.log(jnp.sum(jnp.exp(scores - row_top[:, None]), axis=1))
    probs = jnp.where(allowed, jnp.exp(scores - log_total[:, None]), 0.0)
    attn_rows = jnp.dot(probs.astype(low), value_rows, preferred_element_type=jnp.float32)
    attn_rows = attn_rows.astype(low)
    row_delta = jnp.sum(cotangent.astype(jnp.float32) * attn_rows.astype(jnp.float32), axis=1)

    stats = spread(jnp.stack([log_total, row_delta]), ctx_axes, ctx_count)
    stats = stats.reshape(z_count, 2, 2, 2, row_count)
    stats = jnp.where(x_lo == 1, stats[:, ::-1], stats)
    stats = jnp.where(core == 1, stats[:, :, ::-1], stats)
    stats = stats.transpose(3, 2, 1, 0, 4).reshape(2, ctx_count * row_count)
    total_all, delta_all = stats[0], stats[1]

    dprob = contract_last(cotangent, value_rows)
    dscore = probs * (dprob - row_delta[:, None] + 2.0 * z_weight * log_total[:, None])
    grad_query = jnp.dot(dscore.astype(low), key_rows, preferred_element_type=jnp.float32)
    grad_query = (grad_query * score_scale).astype(low)

    allowed_back = own_positions[:, None] <= all_positions[None, :]
    scores_back = jnp.where(
        allowed_back, contract_last(own_keys, query_all) * score_scale, masked_fill
    )
    probs_back = jnp.where(allowed_back, jnp.exp(scores_back - total_all[None, :]), 0.0)
    dprob_back = contract_last(own_values, cotangent_all)
    dscore_back = probs_back * (
        dprob_back - delta_all[None, :] + 2.0 * z_weight * total_all[None, :]
    )
    grad_key = jnp.dot(dscore_back.astype(low), query_all, preferred_element_type=jnp.float32)
    grad_key = (grad_key * score_scale).astype(low)
    grad_value = jnp.dot(
        probs_back.astype(low), cotangent_all, preferred_element_type=jnp.float32
    ).astype(low)
    grad_rows = jnp.concatenate([grad_query, grad_key, grad_value], axis=1)

    grad_all = spread(grad_rows, "y", y_count).reshape(y_count * row_count, width)
    partial_sum = contract_first(columns, grad_all).astype(low)
    pieces = exchange(
        partial_sum.reshape(2 * ctx_count, shard // ctx_count, width), ("xh",) + ctx_axes
    )
    own_piece = jnp.sum(pieces.astype(jnp.float32), axis=0).astype(low)
    weight_total = spread(own_piece, ctx_axes, ctx_count).reshape(shard, width)
    return (attn_rows[None], weight_total)


def solution(mesh):
    grid = Mesh(mesh.devices.reshape(2, 8, 8, 2, 2), ("xh", "y") + ctx_axes)
    rows, weights = P(("xh", "y"), ctx_axes, None), P(("xh", "y"), None)
    return jax.shard_map(
        on_device,
        mesh=grid,
        in_specs=(rows, weights, rows),
        out_specs=(rows, weights),
        check_vma=False,
    )
```

```python
import functools
import math

import jax
import jax.numpy as jnp
from jax import lax
from jax.experimental import pallas as pl
from jax.experimental.pallas import tpu as pltpu
from jax.sharding import Mesh, PartitionSpec as P

z_weight = 0.001
masked_fill = -1e30
low = jnp.bfloat16
z_axes = ("zh", "zl")
ctx_axes = z_axes + ("xl", "core")
group_axes = ("xh", "zl")
vmem = pltpu.CompilerParams(vmem_limit_bytes=32 * 1024 * 1024)


def dot_f32(left, right, left_dim, right_dim):
    return lax.dot_general(
        left, right, (((left_dim,), (right_dim,)), ((), ())), preferred_element_type=jnp.float32
    )


def exchange(blocks, axes):
    return lax.all_to_all(blocks, axes, split_axis=0, concat_axis=0, tiled=True)


def spread(block, axes, count):
    return exchange(jnp.broadcast_to(block[None], (count,) + block.shape), axes)


def swap(block, axis):
    return lax.ppermute(block, axis, ((0, 1), (1, 0)))


def gather_pieces(block):
    along_z = spread(block, z_axes, lax.axis_size(z_axes))
    along_z = along_z.reshape(-1, block.shape[1])
    by_x = swap(along_z, "xl")
    return along_z, by_x, swap(along_z, "core"), swap(by_x, "core")


def positions(device, inside, half_rows, ctx_count):
    block = jnp.where(inside < half_rows, device, 2 * ctx_count - 1 - device)
    return block * half_rows + inside % half_rows


def piece_device(piece, z):
    return z * 4 + (lax.axis_index("xl") ^ (piece & 1)) * 2 + (lax.axis_index("core") ^ (piece >> 1))


def forward_kernel(
    z_count, q_ref, kv0, kv1, kv2, kv3, cot_ref, attn_ref, stats_ref, dq_ref, held
):
    pieces = (kv0, kv1, kv2, kv3)
    rows, head = q_ref.shape
    half_rows, ctx_count = rows // 2, 4 * z_count
    scale = 1.0 / math.sqrt(head)
    own = piece_device(0, lax.axis_index(z_axes))
    down = lax.broadcasted_iota(jnp.int32, (rows, rows), 0)
    across = lax.broadcasted_iota(jnp.int32, (rows, rows), 1)
    own_positions = positions(own, down, half_rows, ctx_count)
    queries, cotangent = q_ref[...], cot_ref[...]
    top = None
    for piece, kv in enumerate(pieces):
        raw = dot_f32(queries, kv[:, :head], 1, 1) * scale
        for z in range(z_count):
            device = piece_device(piece, z)
            allowed = positions(device, across, half_rows, ctx_count) <= own_positions
            tile = jnp.where(allowed, raw[:, z * rows : (z + 1) * rows], masked_fill)
            held[piece, :, z * rows : (z + 1) * rows] = tile
            top = tile if top is None else jnp.maximum(top, tile)
    row_top = jnp.max(top, axis=1, keepdims=True)
    total = jnp.zeros((rows, rows), jnp.float32)
    for piece in range(4):
        weights = jnp.exp(held[piece] - row_top)
        held[piece] = weights
        for z in range(z_count):
            total = total + weights[:, z * rows : (z + 1) * rows]
    row_sum = jnp.sum(total, axis=1, keepdims=True)
    inverse = 1.0 / row_sum
    log_total = row_top + jnp.log(row_sum)
    attn = jnp.zeros((rows, head), jnp.float32)
    for piece, kv in enumerate(pieces):
        attn = attn + dot_f32((held[piece] * inverse).astype(low), kv[:, head:], 1, 0)
    attn_low = attn.astype(low)
    attn_ref[...] = attn_low
    delta = jnp.sum(
        cotangent.astype(jnp.float32) * attn_low.astype(jnp.float32), axis=1, keepdims=True
    )
    shift = 2.0 * z_weight * log_total - delta
    stats_ref[0:1, :] = jnp.transpose(jnp.broadcast_to(log_total, (rows, rows)))[0:1, :]
    stats_ref[1:2, :] = jnp.transpose(jnp.broadcast_to(shift, (rows, rows)))[0:1, :]
    grad = jnp.zeros((rows, head), jnp.float32)
    for piece, kv in enumerate(pieces):
        dprob = dot_f32(cotangent, kv[:, head:], 1, 1)
        dscore = held[piece] * inverse * (dprob + shift)
        grad = grad + dot_f32(dscore.astype(low), kv[:, :head], 1, 0)
    dq_ref[...] = (grad * scale).astype(low)


def backward_kernel(z_count, kv_ref, qc0, qc1, qc2, qc3, stats_ref, out_ref):
    rows, head = kv_ref.shape[0], kv_ref.shape[1] // 2
    half_rows, ctx_count = rows // 2, 4 * z_count
    scale = 1.0 / math.sqrt(head)
    own = piece_device(0, lax.axis_index(z_axes))
    down = lax.broadcasted_iota(jnp.int32, (rows, rows), 0)
    across = lax.broadcasted_iota(jnp.int32, (rows, rows), 1)
    own_positions = positions(own, down, half_rows, ctx_count)
    keys, values = kv_ref[:, :head], kv_ref[:, head:]
    grad_key = jnp.zeros((rows, head), jnp.float32)
    grad_value = jnp.zeros((rows, head), jnp.float32)
    for piece, both in enumerate((qc0, qc1, qc2, qc3)):
        slot = piece_device(piece, 0)
        queries, cotangent = both[:, :head], both[:, head:]
        scores = dot_f32(keys, queries, 1, 1) * scale
        dprob = dot_f32(values, cotangent, 1, 1)
        probs, dscores = [], []
        for z in range(z_count):
            span = slice(z * rows, (z + 1) * rows)
            stats = stats_ref[4 * z + slot]
            device = piece_device(piece, z)
            allowed = own_positions <= positions(device, across, half_rows, ctx_count)
            masked = jnp.where(allowed, scores[:, span], masked_fill)
            prob = jnp.exp(masked - stats[0:1, :])
            probs.append(prob.astype(low))
            dscores.append((prob * (dprob[:, span] + stats[1:2, :])).astype(low))
        grad_value = grad_value + dot_f32(jnp.concatenate(probs, axis=1), cotangent, 1, 0)
        grad_key = grad_key + dot_f32(jnp.concatenate(dscores, axis=1), queries, 1, 0)
    out_ref[:, :head] = (grad_key * scale).astype(low)
    out_ref[:, head:] = grad_value.astype(low)


def flipped(distance):
    return (lax.axis_index("xh") * 2 + lax.axis_index("zl")) ^ distance


def relayout_kernel(y_count, tokens_ref, out0, out1, out2, out3, sems):
    shard = tokens_ref.shape[1] // (2 * y_count)
    quarter = shard // 4
    core = lax.axis_index("core")
    copies = []
    for distance, out in enumerate((out0, out1, out2, out3)):
        member = flipped(distance)
        for half in range(2):
            for y in range(y_count):
                start = ((member // 2) * y_count + y) * shard
                start = start + ((member % 2) * 2 + (core ^ half)) * quarter
                source = tokens_ref.at[:, pl.ds(pl.multiple_of(start, quarter), quarter)]
                target = out.at[:, pl.ds((half * y_count + y) * quarter, quarter)]
                copies.append(pltpu.make_async_copy(source, target, sems.at[len(copies)]))
    for copy in copies:
        copy.start()
    for copy in copies:
        copy.wait()


def near_kernel(x0, x1, x2, x3, weight_ref, out_ref):
    for distance, x in enumerate((x0, x1, x2, x3)):
        out_ref[distance] = dot_f32(x[...], weight_ref[...], 1, 0)


def far_kernel(x0, x1, x2, x3, weight_ref, sum_ref, out_ref):
    for distance, x in enumerate((x0, x1, x2, x3)):
        total = sum_ref[distance] + dot_f32(x[...], weight_ref[...], 1, 0)
        out_ref[flipped(distance)] = total.astype(low)


def weight_kernel(x0, x1, x2, x3, grad_ref, out_ref):
    rows = jnp.concatenate([x0[...], x1[...], x2[...], x3[...]], axis=0)
    grads = jnp.concatenate([grad_ref[flipped(distance)] for distance in range(4)], axis=0)
    out_ref[...] = dot_f32(rows, grads, 0, 0).astype(out_ref.dtype)


def in_vmem(count):
    return [pl.BlockSpec(memory_space=pltpu.VMEM)] * count


def on_device(tokens, qkv_weight, out_grad):
    y_count, z_count = lax.axis_size("y"), lax.axis_size(z_axes)
    ctx_count = z_count * 4
    row_count, model, width = tokens.shape[1], tokens.shape[2], qkv_weight.shape[1]
    shard, head = qkv_weight.shape[0], qkv_weight.shape[1] // 3
    quarter, depth = shard // 4, model // 8
    cotangent = out_grad[0]

    at = (lax.axis_index("zl") * 2 + lax.axis_index("core")) * quarter
    near = spread(lax.dynamic_slice_in_dim(qkv_weight, at, quarter), "y", y_count)
    near = near.reshape(depth, width)
    x0, x1, x2, x3 = pl.pallas_call(
        functools.partial(relayout_kernel, y_count),
        in_specs=[pl.BlockSpec(memory_space=pl.ANY)],
        out_specs=[pl.BlockSpec(memory_space=pl.ANY)] * 4,
        out_shape=[jax.ShapeDtypeStruct((row_count, 2 * depth), low)] * 4,
        scratch_shapes=[pltpu.SemaphoreType.DMA((8 * y_count,))],
        name="token_columns",
    )(tokens[0])
    columns = (
        x0,
        swap(x1, "zl"),
        swap(x2, "xh"),
        lax.ppermute(x3, group_axes, ((0, 3), (1, 2), (2, 1), (3, 0))),
    )
    near, columns = lax.optimization_barrier((near, columns))
    far = swap(near, "core")

    def column_half(half):
        return [pl.BlockSpec((row_count, depth), lambda i: (0, half))] * 4

    whole_weight = pl.BlockSpec((depth, width), lambda i: (0, 0))
    four_rows = pl.BlockSpec((4, row_count, width), lambda i: (0, 0, 0))
    near_sum = pl.pallas_call(
        near_kernel,
        grid=(1,),
        in_specs=column_half(0) + [whole_weight],
        out_specs=four_rows,
        out_shape=jax.ShapeDtypeStruct((4, row_count, width), jnp.float32),
        compiler_params=vmem,
        name="near_projection",
    )(*columns, near)
    parts = pl.pallas_call(
        far_kernel,
        grid=(1,),
        in_specs=column_half(1) + [whole_weight, four_rows],
        out_specs=four_rows,
        out_shape=jax.ShapeDtypeStruct((4, row_count, width), low),
        compiler_params=vmem,
        name="far_projection",
    )(*columns, far, near_sum)
    parts = exchange(parts, group_axes)
    qkv = jnp.sum(parts.astype(jnp.float32), axis=0).astype(low)
    queries, own_pairs = qkv[:, :head], qkv[:, head:]
    pair_pieces = gather_pieces(own_pairs)
    query_pieces = gather_pieces(jnp.concatenate([queries, cotangent], axis=1))

    attn_rows, stats, grad_query = pl.pallas_call(
        functools.partial(forward_kernel, z_count),
        in_specs=in_vmem(6),
        out_specs=in_vmem(3),
        out_shape=[
            jax.ShapeDtypeStruct((row_count, head), low),
            jax.ShapeDtypeStruct((2, row_count), jnp.float32),
            jax.ShapeDtypeStruct((row_count, head), low),
        ],
        scratch_shapes=[pltpu.VMEM((4, row_count, z_count * row_count), jnp.float32)],
        compiler_params=vmem,
        name="attention_rows",
    )(queries, *pair_pieces, cotangent)

    stats_all = spread(stats, ctx_axes, ctx_count)

    grad_pairs = pl.pallas_call(
        functools.partial(backward_kernel, z_count),
        in_specs=in_vmem(6),
        out_specs=in_vmem(1)[0],
        out_shape=jax.ShapeDtypeStruct((row_count, 2 * head), low),
        compiler_params=vmem,
        name="attention_columns",
    )(own_pairs, *query_pieces, stats_all)

    grad_all = spread(jnp.concatenate([grad_query, grad_pairs], axis=1), group_axes, 4)

    def weight_half(half, dtype):
        return pl.pallas_call(
            weight_kernel,
            grid=(1,),
            in_specs=column_half(half) + [four_rows],
            out_specs=whole_weight,
            out_shape=jax.ShapeDtypeStruct((depth, width), dtype),
            compiler_params=vmem,
            name="weight_gradient",
        )(*columns, grad_all)

    sent = swap(weight_half(1, low), "core")
    summed = (weight_half(0, jnp.float32) + sent.astype(jnp.float32)).astype(low)
    pieces = exchange(summed.reshape(8 * y_count, -1, width), ("y", "zh", "xl"))
    own_piece = jnp.sum(pieces.astype(jnp.float32), axis=0).astype(low)
    total = spread(own_piece, ctx_axes, ctx_count)
    total = total.reshape((z_count // 2, 2, 2, 2) + own_piece.shape).transpose(1, 3, 0, 2, 4, 5)
    return (attn_rows[None], total.reshape(shard, width))


def solution(mesh):
    grid = Mesh(mesh.devices.reshape(2, 8, 4, 2, 2, 2), ("xh", "y") + ctx_axes)
    rows, weights = P(("xh", "y"), ctx_axes, None), P(("xh", "y"), None)
    return jax.shard_map(
        on_device,
        mesh=grid,
        in_specs=(rows, weights, rows),
        out_specs=(rows, weights),
        check_vma=False,
    )
```

```python
import functools
import math

import jax
import jax.numpy as jnp
from jax import lax
from jax.experimental import pallas as pl
from jax.experimental.pallas import tpu as pltpu
from jax.sharding import Mesh, PartitionSpec as P

z_weight = 0.001
masked_fill = -1e30
low = jnp.bfloat16
z_axes = ("zh", "zl")
ctx_axes = z_axes + ("xl", "core")
group_axes = ("xh", "yl", "zl")
vmem = pltpu.CompilerParams(vmem_limit_bytes=32 * 1024 * 1024)


def dot_f32(left, right, left_dim, right_dim):
    return lax.dot_general(
        left, right, (((left_dim,), (right_dim,)), ((), ())), preferred_element_type=jnp.float32
    )


def exchange(blocks, axes):
    return lax.all_to_all(blocks, axes, split_axis=0, concat_axis=0, tiled=True)


def spread(block, axes, count):
    return exchange(jnp.broadcast_to(block[None], (count,) + block.shape), axes)


def swap(block, axis):
    return lax.ppermute(block, axis, ((0, 1), (1, 0)))


def gather_x(block):
    along_z = spread(block, z_axes, lax.axis_size(z_axes)).reshape(-1, block.shape[1])
    return along_z, swap(along_z, "xl")


def positions(device, inside, half_rows, ctx_count):
    block = jnp.where(inside < half_rows, device, 2 * ctx_count - 1 - device)
    return block * half_rows + inside % half_rows


def piece_device(piece, z):
    return z * 4 + (lax.axis_index("xl") ^ (piece & 1)) * 2 + (lax.axis_index("core") ^ (piece >> 1))


def forward_kernel(
    z_count, q_ref, kv0, kv1, kv2, kv3, cot_ref, attn_ref, stats_ref, dq_ref, held
):
    pieces = (kv0, kv1, kv2, kv3)
    rows, head = q_ref.shape
    half_rows, ctx_count = rows // 2, 4 * z_count
    scale = 1.0 / math.sqrt(head)
    own = piece_device(0, lax.axis_index(z_axes))
    down = lax.broadcasted_iota(jnp.int32, (rows, rows), 0)
    across = lax.broadcasted_iota(jnp.int32, (rows, rows), 1)
    own_positions = positions(own, down, half_rows, ctx_count)
    queries, cotangent = q_ref[...], cot_ref[...]
    top = None
    for piece, kv in enumerate(pieces):
        raw = dot_f32(queries, kv[:, :head], 1, 1) * scale
        for z in range(z_count):
            device = piece_device(piece, z)
            allowed = positions(device, across, half_rows, ctx_count) <= own_positions
            tile = jnp.where(allowed, raw[:, z * rows : (z + 1) * rows], masked_fill)
            held[piece, :, z * rows : (z + 1) * rows] = tile
            top = tile if top is None else jnp.maximum(top, tile)
    row_top = jnp.max(top, axis=1, keepdims=True)
    total = jnp.zeros((rows, rows), jnp.float32)
    for piece in range(4):
        weights = jnp.exp(held[piece] - row_top)
        held[piece] = weights
        for z in range(z_count):
            total = total + weights[:, z * rows : (z + 1) * rows]
    row_sum = jnp.sum(total, axis=1, keepdims=True)
    inverse = 1.0 / row_sum
    log_total = row_top + jnp.log(row_sum)
    attn = jnp.zeros((rows, head), jnp.float32)
    for piece, kv in enumerate(pieces):
        attn = attn + dot_f32((held[piece] * inverse).astype(low), kv[:, head:], 1, 0)
    attn_low = attn.astype(low)
    attn_ref[...] = attn_low
    delta = jnp.sum(
        cotangent.astype(jnp.float32) * attn_low.astype(jnp.float32), axis=1, keepdims=True
    )
    shift = 2.0 * z_weight * log_total - delta
    stats_ref[0:1, :] = jnp.transpose(jnp.broadcast_to(log_total, (rows, rows)))[0:1, :]
    stats_ref[1:2, :] = jnp.transpose(jnp.broadcast_to(shift, (rows, rows)))[0:1, :]
    grad = jnp.zeros((rows, head), jnp.float32)
    for piece, kv in enumerate(pieces):
        dprob = dot_f32(cotangent, kv[:, head:], 1, 1)
        dscore = held[piece] * inverse * (dprob + shift)
        grad = grad + dot_f32(dscore.astype(low), kv[:, :head], 1, 0)
    dq_ref[...] = (grad * scale).astype(low)


def backward_kernel(z_count, kv_ref, qc0, qc1, qc2, qc3, stats_ref, out_ref):
    rows, head = kv_ref.shape[0], kv_ref.shape[1] // 2
    half_rows, ctx_count = rows // 2, 4 * z_count
    scale = 1.0 / math.sqrt(head)
    own = piece_device(0, lax.axis_index(z_axes))
    down = lax.broadcasted_iota(jnp.int32, (rows, rows), 0)
    across = lax.broadcasted_iota(jnp.int32, (rows, rows), 1)
    own_positions = positions(own, down, half_rows, ctx_count)
    keys, values = kv_ref[:, :head], kv_ref[:, head:]
    grad_key = jnp.zeros((rows, head), jnp.float32)
    grad_value = jnp.zeros((rows, head), jnp.float32)
    for piece, both in enumerate((qc0, qc1, qc2, qc3)):
        slot = piece_device(piece, 0)
        queries, cotangent = both[:, :head], both[:, head:]
        scores = dot_f32(keys, queries, 1, 1) * scale
        dprob = dot_f32(values, cotangent, 1, 1)
        probs, dscores = [], []
        for z in range(z_count):
            span = slice(z * rows, (z + 1) * rows)
            stats = stats_ref[4 * z + slot]
            device = piece_device(piece, z)
            allowed = own_positions <= positions(device, across, half_rows, ctx_count)
            masked = jnp.where(allowed, scores[:, span], masked_fill)
            prob = jnp.exp(masked - stats[0:1, :])
            probs.append(prob.astype(low))
            dscores.append((prob * (dprob[:, span] + stats[1:2, :])).astype(low))
        grad_value = grad_value + dot_f32(jnp.concatenate(probs, axis=1), cotangent, 1, 0)
        grad_key = grad_key + dot_f32(jnp.concatenate(dscores, axis=1), queries, 1, 0)
    out_ref[:, :head] = (grad_key * scale).astype(low)
    out_ref[:, head:] = grad_value.astype(low)


def shard_row(step, count):
    return lax.rem(lax.axis_index("yh") + count - step, count)


def relayout_kernel(y_half, tokens_ref, out_ref):
    members, _, columns = out_ref.shape
    quarter = columns // (2 * y_half)
    core = lax.axis_index("core")
    for member in range(members):
        x_hi, y_lo, z_lo = member // 4, member // 2 % 2, member % 2
        for half in range(2):
            for step in range(y_half):
                shard = (x_hi * y_half + shard_row(step, y_half)) * 2 + y_lo
                start = (shard * 4 + z_lo * 2 + (core ^ half)) * quarter
                target = (half * y_half + step) * quarter
                out_ref[member, :, target : target + quarter] = tokens_ref[
                    :, pl.ds(pl.multiple_of(start, quarter), quarter)
                ]


def project_kernel(x_ref, near_ref, far_ref, out_ref):
    depth = near_ref.shape[0]
    total = dot_f32(x_ref[:, :depth], near_ref[...], 1, 0)
    total = total + dot_f32(x_ref[:, depth:], far_ref[...], 1, 0)
    out_ref[...] = total.astype(low)


def weight_kernel(y_half, x_ref, grad_ref, out_ref):
    total = dot_f32(x_ref[...], grad_ref[...], 0, 0).astype(out_ref.dtype)
    quarter = total.shape[0] // y_half
    for step in range(y_half):
        out_ref[shard_row(step, y_half)] = total[step * quarter : (step + 1) * quarter]


def in_vmem(count):
    return [pl.BlockSpec(memory_space=pltpu.VMEM)] * count


def on_device(tokens, qkv_weight, out_grad):
    y_half, z_count = lax.axis_size("yh"), lax.axis_size(z_axes)
    ctx_count = z_count * 4
    row_count, model, width = tokens.shape[1], tokens.shape[2], qkv_weight.shape[1]
    shard, head = qkv_weight.shape[0], qkv_weight.shape[1] // 3
    quarter, depth, group_rows = shard // 4, model // 16, 8 * row_count
    cotangent = out_grad[0]

    at = (lax.axis_index("zl") * 2 + lax.axis_index("core")) * quarter
    own_weight = lax.dynamic_slice_in_dim(qkv_weight, at, quarter)
    steps = [own_weight]
    for step in range(1, y_half):
        ring = [(i, (i + step) % y_half) for i in range(y_half)]
        steps.append(lax.ppermute(own_weight, "yh", ring))
    near = jnp.concatenate(steps)
    far = swap(near, "core")
    split = pl.pallas_call(
        functools.partial(relayout_kernel, y_half),
        in_specs=in_vmem(1),
        out_specs=in_vmem(1)[0],
        out_shape=jax.ShapeDtypeStruct((8, row_count, 2 * depth), low),
        compiler_params=vmem,
        name="token_columns",
    )(tokens[0])
    columns = exchange(split, group_axes).reshape(group_rows, 2 * depth)
    parts = pl.pallas_call(
        project_kernel,
        in_specs=in_vmem(3),
        out_specs=in_vmem(1)[0],
        out_shape=jax.ShapeDtypeStruct((group_rows, width), low),
        compiler_params=vmem,
        name="partial_projection",
    )(columns, near, far)
    parts = exchange(parts.reshape(8, row_count, width), group_axes)
    qkv = jnp.sum(parts.astype(jnp.float32), axis=0).astype(low)
    queries, own_pairs = qkv[:, :head], qkv[:, head:]
    pair_pieces = gather_x(own_pairs)
    pair_pieces = pair_pieces + tuple(swap(p, "core") for p in pair_pieces)
    query_pieces = gather_x(jnp.concatenate([queries, cotangent], axis=1))

    attn_rows, stats, grad_query = pl.pallas_call(
        functools.partial(forward_kernel, z_count),
        in_specs=in_vmem(6),
        out_specs=in_vmem(3),
        out_shape=[
            jax.ShapeDtypeStruct((row_count, head), low),
            jax.ShapeDtypeStruct((2, row_count), jnp.float32),
            jax.ShapeDtypeStruct((row_count, head), low),
        ],
        scratch_shapes=[pltpu.VMEM((4, row_count, z_count * row_count), jnp.float32)],
        compiler_params=vmem,
        name="attention_rows",
    )(queries, *pair_pieces, cotangent)

    query_pieces, stats = lax.optimization_barrier((query_pieces, stats))
    query_pieces = query_pieces + tuple(swap(p, "core") for p in query_pieces)
    stats_all = spread(stats, ctx_axes, ctx_count)

    grad_pairs = pl.pallas_call(
        functools.partial(backward_kernel, z_count),
        in_specs=in_vmem(6),
        out_specs=in_vmem(1)[0],
        out_shape=jax.ShapeDtypeStruct((row_count, 2 * head), low),
        compiler_params=vmem,
        name="attention_columns",
    )(own_pairs, *query_pieces, stats_all)

    grad_all = spread(jnp.concatenate([grad_query, grad_pairs], axis=1), group_axes, 8)
    grad_all = grad_all.reshape(group_rows, width)

    def weight_half(half, dtype):
        return pl.pallas_call(
            functools.partial(weight_kernel, y_half),
            grid=(1,),
            in_specs=[
                pl.BlockSpec((group_rows, depth), lambda i: (0, half)),
                pl.BlockSpec((group_rows, width), lambda i: (0, 0)),
            ],
            out_specs=pl.BlockSpec((y_half, quarter, width), lambda i: (0, 0, 0)),
            out_shape=jax.ShapeDtypeStruct((y_half, quarter, width), dtype),
            compiler_params=vmem,
            name="weight_gradient",
        )(columns, grad_all)

    sent = swap(weight_half(1, low), "core")
    summed = (weight_half(0, jnp.float32) + sent.astype(jnp.float32)).astype(low)
    pieces = exchange(summed.reshape(8 * y_half, -1, width), ("yh", "zh", "xl"))
    own_piece = jnp.sum(pieces.astype(jnp.float32), axis=0).astype(low)
    total = spread(own_piece, ctx_axes, ctx_count)
    total = total.reshape((z_count // 2, 2, 2, 2) + own_piece.shape).transpose(1, 3, 0, 2, 4, 5)
    return (attn_rows[None], total.reshape(shard, width))


def solution(mesh):
    grid = Mesh(mesh.devices.reshape(2, 4, 2, 4, 2, 2, 2), ("xh", "yh", "yl") + ctx_axes)
    rows, weights = P(("xh", "yh", "yl"), ctx_axes, None), P(("xh", "yh", "yl"), None)
    return jax.shard_map(
        on_device,
        mesh=grid,
        in_specs=(rows, weights, rows),
        out_specs=(rows, weights),
        check_vma=False,
    )
```

```python
import functools
import math

import jax
import jax.numpy as jnp
from jax import lax
from jax.experimental import pallas as pl
from jax.experimental.pallas import tpu as pltpu
from jax.sharding import Mesh, PartitionSpec as P

z_weight = 0.001
masked_fill = -1e30
low = jnp.bfloat16
z_axes = ("zh", "zl")
ctx_axes = z_axes + ("xl", "core")
group_axes = ("xh", "yl", "zl")
vmem = pltpu.CompilerParams(vmem_limit_bytes=32 * 1024 * 1024)


def dot_f32(left, right, left_dim, right_dim):
    return lax.dot_general(
        left, right, (((left_dim,), (right_dim,)), ((), ())), preferred_element_type=jnp.float32
    )


def exchange(blocks, axes):
    return lax.all_to_all(blocks, axes, split_axis=0, concat_axis=0, tiled=True)


def spread(block, axes, count):
    return exchange(jnp.broadcast_to(block[None], (count,) + block.shape), axes)


def swap(block, axis):
    return lax.ppermute(block, axis, ((0, 1), (1, 0)))


def gather_x(block):
    along_z = spread(block, z_axes, lax.axis_size(z_axes)).reshape(-1, block.shape[1])
    return along_z, swap(along_z, "xl")


def positions(device, inside, half_rows, ctx_count):
    block = jnp.where(inside < half_rows, device, 2 * ctx_count - 1 - device)
    return block * half_rows + inside % half_rows


def piece_device(piece, z):
    return z * 4 + (lax.axis_index("xl") ^ (piece & 1)) * 2 + (lax.axis_index("core") ^ (piece >> 1))


def forward_kernel(
    z_count, q_ref, kv0, kv1, kv2, kv3, cot_ref, attn_ref, stats_ref, dq_ref, held
):
    pieces = (kv0, kv1, kv2, kv3)
    rows, head = q_ref.shape
    half_rows, ctx_count = rows // 2, 4 * z_count
    scale = 1.0 / math.sqrt(head)
    own = piece_device(0, lax.axis_index(z_axes))
    down = lax.broadcasted_iota(jnp.int32, (rows, rows), 0)
    across = lax.broadcasted_iota(jnp.int32, (rows, rows), 1)
    own_positions = positions(own, down, half_rows, ctx_count)
    queries, cotangent = q_ref[...], cot_ref[...]
    top = None
    for piece, kv in enumerate(pieces):
        raw = dot_f32(queries, kv[:, :head], 1, 1) * scale
        for z in range(z_count):
            device = piece_device(piece, z)
            allowed = positions(device, across, half_rows, ctx_count) <= own_positions
            tile = jnp.where(allowed, raw[:, z * rows : (z + 1) * rows], masked_fill)
            held[piece, :, z * rows : (z + 1) * rows] = tile
            top = tile if top is None else jnp.maximum(top, tile)
    row_top = jnp.max(top, axis=1, keepdims=True)
    total = jnp.zeros((rows, rows), jnp.float32)
    for piece in range(4):
        weights = jnp.exp(held[piece] - row_top)
        held[piece] = weights
        for z in range(z_count):
            total = total + weights[:, z * rows : (z + 1) * rows]
    row_sum = jnp.sum(total, axis=1, keepdims=True)
    inverse = 1.0 / row_sum
    log_total = row_top + jnp.log(row_sum)
    attn = jnp.zeros((rows, head), jnp.float32)
    for piece, kv in enumerate(pieces):
        attn = attn + dot_f32((held[piece] * inverse).astype(low), kv[:, head:], 1, 0)
    attn_low = attn.astype(low)
    attn_ref[...] = attn_low
    delta = jnp.sum(
        cotangent.astype(jnp.float32) * attn_low.astype(jnp.float32), axis=1, keepdims=True
    )
    shift = 2.0 * z_weight * log_total - delta
    stats_ref[0:1, :] = jnp.transpose(jnp.broadcast_to(log_total, (rows, rows)))[0:1, :]
    stats_ref[1:2, :] = jnp.transpose(jnp.broadcast_to(shift, (rows, rows)))[0:1, :]
    grad = jnp.zeros((rows, head), jnp.float32)
    for piece, kv in enumerate(pieces):
        dprob = dot_f32(cotangent, kv[:, head:], 1, 1)
        dscore = held[piece] * inverse * (dprob + shift)
        grad = grad + dot_f32(dscore.astype(low), kv[:, :head], 1, 0)
    dq_ref[...] = (grad * scale).astype(low)


def backward_kernel(z_count, kv_ref, q0, q1, q2, q3, cot_ref, stats_ref, out_ref):
    rows, head = kv_ref.shape[0], kv_ref.shape[1] // 2
    half_rows, ctx_count = rows // 2, 4 * z_count
    scale = 1.0 / math.sqrt(head)
    own = piece_device(0, lax.axis_index(z_axes))
    down = lax.broadcasted_iota(jnp.int32, (rows, rows), 0)
    across = lax.broadcasted_iota(jnp.int32, (rows, rows), 1)
    own_positions = positions(own, down, half_rows, ctx_count)
    keys, values = kv_ref[:, :head], kv_ref[:, head:]
    grad_key = jnp.zeros((rows, head), jnp.float32)
    grad_value = jnp.zeros((rows, head), jnp.float32)
    for piece, queries_ref in enumerate((q0, q1, q2, q3)):
        slot = piece_device(piece, 0)
        queries = queries_ref[...]
        cotangent = jnp.concatenate([cot_ref[4 * z + slot] for z in range(z_count)], axis=0)
        scores = dot_f32(keys, queries, 1, 1) * scale
        dprob = dot_f32(values, cotangent, 1, 1)
        probs, dscores = [], []
        for z in range(z_count):
            span = slice(z * rows, (z + 1) * rows)
            stats = stats_ref[4 * z + slot]
            device = piece_device(piece, z)
            allowed = own_positions <= positions(device, across, half_rows, ctx_count)
            masked = jnp.where(allowed, scores[:, span], masked_fill)
            prob = jnp.exp(masked - stats[0:1, :])
            probs.append(prob.astype(low))
            dscores.append((prob * (dprob[:, span] + stats[1:2, :])).astype(low))
        grad_value = grad_value + dot_f32(jnp.concatenate(probs, axis=1), cotangent, 1, 0)
        grad_key = grad_key + dot_f32(jnp.concatenate(dscores, axis=1), queries, 1, 0)
    out_ref[:, :head] = (grad_key * scale).astype(low)
    out_ref[:, head:] = grad_value.astype(low)


def shard_row(step, count):
    return lax.rem(lax.axis_index("yh") + count - step, count)


def relayout_kernel(y_half, tokens_ref, out_ref):
    members, _, columns = out_ref.shape
    quarter = columns // (2 * y_half)
    core = lax.axis_index("core")
    for member in range(members):
        x_hi, y_lo, z_lo = member // 4, member // 2 % 2, member % 2
        for half in range(2):
            for step in range(y_half):
                shard = (x_hi * y_half + shard_row(step, y_half)) * 2 + y_lo
                start = (shard * 4 + z_lo * 2 + (core ^ half)) * quarter
                target = (half * y_half + step) * quarter
                out_ref[member, :, target : target + quarter] = tokens_ref[
                    :, pl.ds(pl.multiple_of(start, quarter), quarter)
                ]


def project_kernel(x_ref, near_ref, far_ref, out_ref):
    depth = near_ref.shape[0]
    total = dot_f32(x_ref[:, :depth], near_ref[...], 1, 0)
    total = total + dot_f32(x_ref[:, depth:], far_ref[...], 1, 0)
    out_ref[...] = total.astype(low)


def weight_kernel(y_half, x_ref, grad_ref, out_ref):
    total = dot_f32(x_ref[...], grad_ref[...], 0, 0).astype(out_ref.dtype)
    quarter = total.shape[0] // y_half
    for step in range(y_half):
        out_ref[shard_row(step, y_half)] = total[step * quarter : (step + 1) * quarter]


def in_vmem(count):
    return [pl.BlockSpec(memory_space=pltpu.VMEM)] * count


def on_device(tokens, qkv_weight, out_grad):
    y_half, z_count = lax.axis_size("yh"), lax.axis_size(z_axes)
    ctx_count = z_count * 4
    row_count, model, width = tokens.shape[1], tokens.shape[2], qkv_weight.shape[1]
    shard, head = qkv_weight.shape[0], qkv_weight.shape[1] // 3
    quarter, depth, group_rows = shard // 4, model // 16, 8 * row_count
    cotangent = out_grad[0]

    x_lo, half_quarter = lax.axis_index("xl"), quarter // 2
    at = (lax.axis_index("zl") * 2 + lax.axis_index("core")) * quarter + x_lo * half_quarter
    own_weight = lax.dynamic_slice_in_dim(qkv_weight, at, half_quarter)
    steps = [own_weight]
    for step in range(1, y_half):
        ring = [(i, (i + step) % y_half) for i in range(y_half)]
        steps.append(lax.ppermute(own_weight, "yh", ring))
    fetched = jnp.stack(steps)
    other = swap(fetched, "xl")
    near = jnp.where(
        x_lo == 0,
        jnp.concatenate([fetched, other], axis=1),
        jnp.concatenate([other, fetched], axis=1),
    ).reshape(depth, width)
    far = swap(near, "core")
    split = pl.pallas_call(
        functools.partial(relayout_kernel, y_half),
        in_specs=in_vmem(1),
        out_specs=in_vmem(1)[0],
        out_shape=jax.ShapeDtypeStruct((8, row_count, 2 * depth), low),
        compiler_params=vmem,
        name="token_columns",
    )(tokens[0])
    columns = exchange(split, group_axes).reshape(group_rows, 2 * depth)
    parts = pl.pallas_call(
        project_kernel,
        in_specs=in_vmem(3),
        out_specs=in_vmem(1)[0],
        out_shape=jax.ShapeDtypeStruct((group_rows, width), low),
        compiler_params=vmem,
        name="partial_projection",
    )(columns, near, far)
    parts = exchange(parts.reshape(8, row_count, width), group_axes)
    qkv = jnp.sum(parts.astype(jnp.float32), axis=0).astype(low)
    queries, own_pairs = qkv[:, :head], qkv[:, head:]
    pair_pieces = gather_x(own_pairs)
    pair_pieces = pair_pieces + tuple(swap(p, "core") for p in pair_pieces)
    query_pieces = gather_x(queries)
    pair_pieces, cotangent_all = lax.optimization_barrier(
        (pair_pieces, lax.all_gather(cotangent, ctx_axes, axis=0, tiled=False))
    )

    attn_rows, stats, grad_query = pl.pallas_call(
        functools.partial(forward_kernel, z_count),
        in_specs=in_vmem(6),
        out_specs=in_vmem(3),
        out_shape=[
            jax.ShapeDtypeStruct((row_count, head), low),
            jax.ShapeDtypeStruct((2, row_count), jnp.float32),
            jax.ShapeDtypeStruct((row_count, head), low),
        ],
        scratch_shapes=[pltpu.VMEM((4, row_count, z_count * row_count), jnp.float32)],
        compiler_params=vmem,
        name="attention_rows",
    )(queries, *pair_pieces, cotangent)

    stats_all = spread(stats, ctx_axes, ctx_count)
    query_pieces, stats_all = lax.optimization_barrier((query_pieces, stats_all))
    query_pieces = query_pieces + tuple(swap(p, "core") for p in query_pieces)

    grad_pairs = pl.pallas_call(
        functools.partial(backward_kernel, z_count),
        in_specs=in_vmem(7),
        out_specs=in_vmem(1)[0],
        out_shape=jax.ShapeDtypeStruct((row_count, 2 * head), low),
        compiler_params=vmem,
        name="attention_columns",
    )(own_pairs, *query_pieces, cotangent_all, stats_all)

    grad_all = spread(jnp.concatenate([grad_query, grad_pairs], axis=1), group_axes, 8)
    grad_all = grad_all.reshape(group_rows, width)

    def weight_half(half, dtype):
        return pl.pallas_call(
            functools.partial(weight_kernel, y_half),
            grid=(1,),
            in_specs=[
                pl.BlockSpec((group_rows, depth), lambda i: (0, half)),
                pl.BlockSpec((group_rows, width), lambda i: (0, 0)),
            ],
            out_specs=pl.BlockSpec((y_half, quarter, width), lambda i: (0, 0, 0)),
            out_shape=jax.ShapeDtypeStruct((y_half, quarter, width), dtype),
            compiler_params=vmem,
            name="weight_gradient",
        )(columns, grad_all)

    sent = swap(weight_half(1, low), "core")
    summed = (weight_half(0, jnp.float32) + sent.astype(jnp.float32)).astype(low)
    pieces = exchange(summed.reshape(8 * y_half, -1, width), ("yh", "zh", "xl"))
    own_piece = jnp.sum(pieces.astype(jnp.float32), axis=0).astype(low)
    on_core = spread(own_piece, z_axes + ("xl",), 2 * z_count)
    on_core = on_core.reshape((z_count // 2, 2, 2) + own_piece.shape).transpose(1, 0, 2, 3, 4)
    across = swap(on_core, "core")
    first = lax.axis_index("core") == 0
    total = jnp.stack([jnp.where(first, on_core, across), jnp.where(first, across, on_core)], axis=1)
    return (attn_rows[None], total.reshape(shard, width))


def solution(mesh):
    grid = Mesh(mesh.devices.reshape(2, 4, 2, 4, 2, 2, 2), ("xh", "yh", "yl") + ctx_axes)
    rows, weights = P(("xh", "yh", "yl"), ctx_axes, None), P(("xh", "yh", "yl"), None)
    return jax.shard_map(
        on_device,
        mesh=grid,
        in_specs=(rows, weights, rows),
        out_specs=(rows, weights),
        check_vma=False,
    )
```

```python
import functools
import math

import jax
import jax.numpy as jnp
from jax import lax
from jax.experimental import pallas as pl
from jax.experimental.pallas import tpu as pltpu
from jax.sharding import Mesh, PartitionSpec as P

z_weight = 0.001
masked_fill = -1e30
low = jnp.bfloat16
z_axes = ("zh", "zl")
ctx_axes = z_axes + ("xl", "core")
group_axes = ("xh", "yl", "zl")
vmem = pltpu.CompilerParams(vmem_limit_bytes=32 * 1024 * 1024)


def dot_f32(left, right, left_dim, right_dim):
    return lax.dot_general(
        left, right, (((left_dim,), (right_dim,)), ((), ())), preferred_element_type=jnp.float32
    )


def exchange(blocks, axes):
    return lax.all_to_all(blocks, axes, split_axis=0, concat_axis=0, tiled=True)


def spread(block, axes, count):
    return exchange(jnp.broadcast_to(block[None], (count,) + block.shape), axes)


def swap(block, axis):
    return lax.ppermute(block, axis, ((0, 1), (1, 0)))


def doubled(blocks, axis, flip):
    pairs = [(i, i ^ flip) for i in range(lax.axis_size(axis))]
    return jnp.concatenate([blocks, lax.ppermute(blocks, axis, pairs)])


def gather_x(block):
    along_z = spread(block, z_axes, lax.axis_size(z_axes)).reshape(-1, block.shape[1])
    return along_z, swap(along_z, "xl")


def positions(device, inside, half_rows, ctx_count):
    block = jnp.where(inside < half_rows, device, 2 * ctx_count - 1 - device)
    return block * half_rows + inside % half_rows


def piece_device(piece, z):
    return z * 4 + (lax.axis_index("xl") ^ (piece & 1)) * 2 + (lax.axis_index("core") ^ (piece >> 1))


def forward_kernel(
    z_count, q_ref, kv0, kv1, kv2, kv3, cot_ref, attn_ref, stats_ref, dq_ref, held
):
    pieces = (kv0, kv1, kv2, kv3)
    rows, head = q_ref.shape
    half_rows, ctx_count = rows // 2, 4 * z_count
    scale = 1.0 / math.sqrt(head)
    own = piece_device(0, lax.axis_index(z_axes))
    down = lax.broadcasted_iota(jnp.int32, (rows, rows), 0)
    across = lax.broadcasted_iota(jnp.int32, (rows, rows), 1)
    own_positions = positions(own, down, half_rows, ctx_count)
    queries, cotangent = q_ref[...], cot_ref[...]
    top = None
    for piece, kv in enumerate(pieces):
        raw = dot_f32(queries, kv[:, :head], 1, 1) * scale
        for z in range(z_count):
            device = piece_device(piece, z)
            allowed = positions(device, across, half_rows, ctx_count) <= own_positions
            tile = jnp.where(allowed, raw[:, z * rows : (z + 1) * rows], masked_fill)
            held[piece, :, z * rows : (z + 1) * rows] = tile
            top = tile if top is None else jnp.maximum(top, tile)
    row_top = jnp.max(top, axis=1, keepdims=True)
    total = jnp.zeros((rows, rows), jnp.float32)
    for piece in range(4):
        weights = jnp.exp(held[piece] - row_top)
        held[piece] = weights
        for z in range(z_count):
            total = total + weights[:, z * rows : (z + 1) * rows]
    row_sum = jnp.sum(total, axis=1, keepdims=True)
    inverse = 1.0 / row_sum
    log_total = row_top + jnp.log(row_sum)
    attn = jnp.zeros((rows, head), jnp.float32)
    for piece, kv in enumerate(pieces):
        attn = attn + dot_f32((held[piece] * inverse).astype(low), kv[:, head:], 1, 0)
    attn_low = attn.astype(low)
    attn_ref[...] = attn_low
    delta = jnp.sum(
        cotangent.astype(jnp.float32) * attn_low.astype(jnp.float32), axis=1, keepdims=True
    )
    shift = 2.0 * z_weight * log_total - delta
    stats_ref[0:1, :] = jnp.transpose(jnp.broadcast_to(log_total, (rows, rows)))[0:1, :]
    stats_ref[1:2, :] = jnp.transpose(jnp.broadcast_to(shift, (rows, rows)))[0:1, :]
    grad = jnp.zeros((rows, head), jnp.float32)
    for piece, kv in enumerate(pieces):
        dprob = dot_f32(cotangent, kv[:, head:], 1, 1)
        dscore = held[piece] * inverse * (dprob + shift)
        grad = grad + dot_f32(dscore.astype(low), kv[:, :head], 1, 0)
    dq_ref[...] = (grad * scale).astype(low)


def backward_kernel(z_count, kv_ref, q0, q1, q2, q3, cot_ref, stats_ref, out_ref):
    rows, head = kv_ref.shape[0], kv_ref.shape[1] // 2
    half_rows, ctx_count = rows // 2, 4 * z_count
    scale = 1.0 / math.sqrt(head)
    z_own = lax.axis_index(z_axes)
    own = piece_device(0, z_own)
    down = lax.broadcasted_iota(jnp.int32, (rows, rows), 0)
    across = lax.broadcasted_iota(jnp.int32, (rows, rows), 1)
    own_positions = positions(own, down, half_rows, ctx_count)
    keys, values = kv_ref[:, :head], kv_ref[:, head:]
    grad_key = jnp.zeros((rows, head), jnp.float32)
    grad_value = jnp.zeros((rows, head), jnp.float32)
    for piece, queries_ref in enumerate((q0, q1, q2, q3)):
        slot = piece_device(piece, 0)
        queries = queries_ref[...]
        cotangent = jnp.concatenate(
            [cot_ref[piece * z_count + (z ^ z_own)] for z in range(z_count)], axis=0
        )
        scores = dot_f32(keys, queries, 1, 1) * scale
        dprob = dot_f32(values, cotangent, 1, 1)
        probs, dscores = [], []
        for z in range(z_count):
            span = slice(z * rows, (z + 1) * rows)
            stats = stats_ref[4 * z + slot]
            device = piece_device(piece, z)
            allowed = own_positions <= positions(device, across, half_rows, ctx_count)
            masked = jnp.where(allowed, scores[:, span], masked_fill)
            prob = jnp.exp(masked - stats[0:1, :])
            probs.append(prob.astype(low))
            dscores.append((prob * (dprob[:, span] + stats[1:2, :])).astype(low))
        grad_value = grad_value + dot_f32(jnp.concatenate(probs, axis=1), cotangent, 1, 0)
        grad_key = grad_key + dot_f32(jnp.concatenate(dscores, axis=1), queries, 1, 0)
    out_ref[:, :head] = (grad_key * scale).astype(low)
    out_ref[:, head:] = grad_value.astype(low)


def relayout_kernel(y_half, tokens_ref, out_ref):
    members, _, columns = out_ref.shape
    quarter = columns // (2 * y_half)
    core = lax.axis_index("core")
    for member in range(members):
        x_hi, y_lo, z_lo = member // 4, member // 2 % 2, member % 2
        for half in range(2):
            for step in range(y_half):
                shard = (x_hi * y_half + step) * 2 + y_lo
                start = (shard * 4 + z_lo * 2 + (core ^ half)) * quarter
                target = (half * y_half + step) * quarter
                out_ref[member, :, target : target + quarter] = tokens_ref[
                    :, pl.ds(pl.multiple_of(start, quarter), quarter)
                ]


def project_kernel(x_ref, near_ref, far_ref, out_ref):
    depth = near_ref.shape[0]
    total = dot_f32(x_ref[:, :depth], near_ref[...], 1, 0)
    total = total + dot_f32(x_ref[:, depth:], far_ref[...], 1, 0)
    out_ref[...] = total.astype(low)


def weight_kernel(x_ref, grad_ref, out_ref):
    out_ref[...] = dot_f32(x_ref[...], grad_ref[...], 0, 0).astype(out_ref.dtype)


def in_vmem(count):
    return [pl.BlockSpec(memory_space=pltpu.VMEM)] * count


def on_device(tokens, qkv_weight, out_grad):
    y_half, z_count = lax.axis_size("yh"), lax.axis_size(z_axes)
    ctx_count = z_count * 4
    row_count, model, width = tokens.shape[1], tokens.shape[2], qkv_weight.shape[1]
    shard, head = qkv_weight.shape[0], qkv_weight.shape[1] // 3
    quarter, depth, group_rows = shard // 4, model // 16, 8 * row_count
    cotangent = out_grad[0]

    at = (lax.axis_index("zl") * 2 + lax.axis_index("core")) * quarter
    own_weight = lax.dynamic_slice_in_dim(qkv_weight, at, quarter)
    near = spread(own_weight, "yh", y_half).reshape(depth, width)
    split = pl.pallas_call(
        functools.partial(relayout_kernel, y_half),
        in_specs=in_vmem(1),
        out_specs=in_vmem(1)[0],
        out_shape=jax.ShapeDtypeStruct((8, row_count, 2 * depth), low),
        compiler_params=vmem,
        name="token_columns",
    )(tokens[0])
    split, near = lax.optimization_barrier((split, near))
    far = swap(near, "core")
    columns = exchange(split, group_axes).reshape(group_rows, 2 * depth)
    cotangent_all = cotangent[None]
    for axis, flip in (("zl", 1), ("zh", 1), ("zh", 2)):
        cotangent_all = doubled(cotangent_all, axis, flip)
    columns, cotangent_all = lax.optimization_barrier((columns, cotangent_all))
    parts = pl.pallas_call(
        project_kernel,
        in_specs=in_vmem(3),
        out_specs=in_vmem(1)[0],
        out_shape=jax.ShapeDtypeStruct((group_rows, width), low),
        compiler_params=vmem,
        name="partial_projection",
    )(columns, near, far)
    parts = exchange(parts.reshape(8, row_count, width), group_axes)
    cotangent_all = doubled(doubled(cotangent_all, "xl", 1), "core", 1)
    parts, cotangent_all = lax.optimization_barrier((parts, cotangent_all))
    qkv = jnp.sum(parts.astype(jnp.float32), axis=0).astype(low)
    queries, own_pairs = qkv[:, :head], qkv[:, head:]
    pair_pieces = gather_x(own_pairs)
    pair_pieces = pair_pieces + tuple(swap(p, "core") for p in pair_pieces)
    query_pieces = gather_x(queries)

    attn_rows, stats, grad_query = pl.pallas_call(
        functools.partial(forward_kernel, z_count),
        in_specs=in_vmem(6),
        out_specs=in_vmem(3),
        out_shape=[
            jax.ShapeDtypeStruct((row_count, head), low),
            jax.ShapeDtypeStruct((2, row_count), jnp.float32),
            jax.ShapeDtypeStruct((row_count, head), low),
        ],
        scratch_shapes=[pltpu.VMEM((4, row_count, z_count * row_count), jnp.float32)],
        compiler_params=vmem,
        name="attention_rows",
    )(queries, *pair_pieces, cotangent)

    stats_all = spread(stats, ctx_axes, ctx_count)
    query_pieces, stats_all = lax.optimization_barrier((query_pieces, stats_all))
    query_pieces = query_pieces + tuple(swap(p, "core") for p in query_pieces)

    grad_pairs = pl.pallas_call(
        functools.partial(backward_kernel, z_count),
        in_specs=in_vmem(7),
        out_specs=in_vmem(1)[0],
        out_shape=jax.ShapeDtypeStruct((row_count, 2 * head), low),
        compiler_params=vmem,
        name="attention_columns",
    )(own_pairs, *query_pieces, cotangent_all, stats_all)

    grad_all = spread(jnp.concatenate([grad_query, grad_pairs], axis=1), group_axes, 8)
    grad_all = grad_all.reshape(group_rows, width)

    def weight_half(half, dtype):
        return pl.pallas_call(
            weight_kernel,
            grid=(1,),
            in_specs=[
                pl.BlockSpec((group_rows, depth), lambda i: (0, half)),
                pl.BlockSpec((group_rows, width), lambda i: (0, 0)),
            ],
            out_specs=pl.BlockSpec((depth, width), lambda i: (0, 0)),
            out_shape=jax.ShapeDtypeStruct((depth, width), dtype),
            compiler_params=vmem,
            name="weight_gradient",
        )(columns, grad_all)

    sent = swap(weight_half(1, low), "core")
    summed = (weight_half(0, jnp.float32) + sent.astype(jnp.float32)).astype(low)
    pieces = exchange(summed.reshape(8 * y_half, -1, width), ("yh", "zh", "xl"))
    own_piece = jnp.sum(pieces.astype(jnp.float32), axis=0).astype(low)
    on_core = spread(own_piece, z_axes + ("xl",), 2 * z_count)
    on_core = on_core.reshape((z_count // 2, 2, 2) + own_piece.shape).transpose(1, 0, 2, 3, 4)
    across = swap(on_core, "core")
    first = lax.axis_index("core") == 0
    total = jnp.stack([jnp.where(first, on_core, across), jnp.where(first, across, on_core)], axis=1)
    return (attn_rows[None], total.reshape(shard, width))


def solution(mesh):
    grid = Mesh(mesh.devices.reshape(2, 4, 2, 4, 2, 2, 2), ("xh", "yh", "yl") + ctx_axes)
    rows, weights = P(("xh", "yh", "yl"), ctx_axes, None), P(("xh", "yh", "yl"), None)
    return jax.shard_map(
        on_device,
        mesh=grid,
        in_specs=(rows, weights, rows),
        out_specs=(rows, weights),
        check_vma=False,
    )
```

```python
import functools
import math

import jax
import jax.numpy as jnp
from jax import lax
from jax.experimental import pallas as pl
from jax.experimental.pallas import tpu as pltpu
from jax.sharding import Mesh, PartitionSpec as P

z_weight = 0.001
masked_fill = -1e30
low = jnp.bfloat16
z_axes = ("zh", "zl")
ctx_axes = z_axes + ("xl", "core")
group_axes = ("xh", "yl", "zl")
vmem = pltpu.CompilerParams(vmem_limit_bytes=32 * 1024 * 1024)


def dot_f32(left, right, left_dim, right_dim):
    return lax.dot_general(
        left, right, (((left_dim,), (right_dim,)), ((), ())), preferred_element_type=jnp.float32
    )


def exchange(blocks, axes):
    return lax.all_to_all(blocks, axes, split_axis=0, concat_axis=0, tiled=True)


def spread(block, axes, count):
    return exchange(jnp.broadcast_to(block[None], (count,) + block.shape), axes)


def swap(block, axis):
    return lax.ppermute(block, axis, ((0, 1), (1, 0)))


def gather_x(block):
    along_z = spread(block, z_axes, lax.axis_size(z_axes)).reshape(-1, block.shape[1])
    return along_z, swap(along_z, "xl")


def positions(device, inside, half_rows, ctx_count):
    block = jnp.where(inside < half_rows, device, 2 * ctx_count - 1 - device)
    return block * half_rows + inside % half_rows


def piece_device(piece, z):
    return z * 4 + (lax.axis_index("xl") ^ (piece & 1)) * 2 + (lax.axis_index("core") ^ (piece >> 1))


def forward_kernel(
    z_count, q_ref, kv0, kv1, kv2, kv3, cot_ref, attn_ref, stats_ref, dq_ref, held
):
    pieces = (kv0, kv1, kv2, kv3)
    rows, head = q_ref.shape
    half_rows, ctx_count = rows // 2, 4 * z_count
    scale = 1.0 / math.sqrt(head)
    own = piece_device(0, lax.axis_index(z_axes))
    down = lax.broadcasted_iota(jnp.int32, (rows, rows), 0)
    across = lax.broadcasted_iota(jnp.int32, (rows, rows), 1)
    own_positions = positions(own, down, half_rows, ctx_count)
    queries, cotangent = q_ref[...], cot_ref[...]
    top = None
    for piece, kv in enumerate(pieces):
        raw = dot_f32(queries, kv[:, :head], 1, 1) * scale
        for z in range(z_count):
            device = piece_device(piece, z)
            allowed = positions(device, across, half_rows, ctx_count) <= own_positions
            tile = jnp.where(allowed, raw[:, z * rows : (z + 1) * rows], masked_fill)
            held[piece, :, z * rows : (z + 1) * rows] = tile
            top = tile if top is None else jnp.maximum(top, tile)
    row_top = jnp.max(top, axis=1, keepdims=True)
    total = jnp.zeros((rows, rows), jnp.float32)
    for piece in range(4):
        weights = jnp.exp(held[piece] - row_top)
        held[piece] = weights
        for z in range(z_count):
            total = total + weights[:, z * rows : (z + 1) * rows]
    row_sum = jnp.sum(total, axis=1, keepdims=True)
    inverse = 1.0 / row_sum
    log_total = row_top + jnp.log(row_sum)
    attn = jnp.zeros((rows, head), jnp.float32)
    for piece, kv in enumerate(pieces):
        attn = attn + dot_f32((held[piece] * inverse).astype(low), kv[:, head:], 1, 0)
    attn_low = attn.astype(low)
    attn_ref[...] = attn_low
    delta = jnp.sum(
        cotangent.astype(jnp.float32) * attn_low.astype(jnp.float32), axis=1, keepdims=True
    )
    shift = 2.0 * z_weight * log_total - delta
    stats_ref[0:1, :] = jnp.transpose(jnp.broadcast_to(log_total, (rows, rows)))[0:1, :]
    stats_ref[1:2, :] = jnp.transpose(jnp.broadcast_to(shift, (rows, rows)))[0:1, :]
    grad = jnp.zeros((rows, head), jnp.float32)
    for piece, kv in enumerate(pieces):
        dprob = dot_f32(cotangent, kv[:, head:], 1, 1)
        dscore = held[piece] * inverse * (dprob + shift)
        grad = grad + dot_f32(dscore.astype(low), kv[:, :head], 1, 0)
    dq_ref[...] = (grad * scale).astype(low)


def backward_kernel(z_count, kv_ref, across_ref, qc0, qc1, stats_ref, own_ref, other_ref):
    rows, head = kv_ref.shape[0], kv_ref.shape[1] // 2
    half_rows, ctx_count = rows // 2, 4 * z_count
    scale = 1.0 / math.sqrt(head)
    z_own = lax.axis_index(z_axes)
    down = lax.broadcasted_iota(jnp.int32, (rows, rows), 0)
    across = lax.broadcasted_iota(jnp.int32, (rows, rows), 1)
    key_positions = jnp.concatenate(
        [
            positions(piece_device(0, z_own), down, half_rows, ctx_count),
            positions(piece_device(2, z_own), down, half_rows, ctx_count),
        ],
        axis=0,
    )
    pairs = jnp.concatenate(
        [kv_ref[...], across_ref[pl.ds(pl.multiple_of(z_own * rows, rows), rows), :]], axis=0
    )
    keys, values = pairs[:, :head], pairs[:, head:]
    grad_key = jnp.zeros((2 * rows, head), jnp.float32)
    grad_value = jnp.zeros((2 * rows, head), jnp.float32)
    for piece, both in enumerate((qc0, qc1)):
        slot = lax.axis_index("xl") ^ piece
        queries, cotangent = both[:, :head], both[:, head:]
        scores = dot_f32(keys, queries, 1, 1) * scale
        dprob = dot_f32(values, cotangent, 1, 1)
        probs, dscores = [], []
        for z in range(z_count):
            span = slice(z * rows, (z + 1) * rows)
            stats = stats_ref[2 * z + slot]
            row_positions = positions(piece_device(piece, z), across, half_rows, ctx_count)
            allowed = key_positions <= jnp.concatenate([row_positions, row_positions], axis=0)
            masked = jnp.where(allowed, scores[:, span], masked_fill)
            prob = jnp.exp(masked - stats[0:1, :])
            probs.append(prob.astype(low))
            dscores.append((prob * (dprob[:, span] + stats[1:2, :])).astype(low))
        grad_value = grad_value + dot_f32(jnp.concatenate(probs, axis=1), cotangent, 1, 0)
        grad_key = grad_key + dot_f32(jnp.concatenate(dscores, axis=1), queries, 1, 0)
    grad_key = grad_key * scale
    own_ref[:, :head], own_ref[:, head:] = grad_key[:rows], grad_value[:rows]
    other_ref[:, :head], other_ref[:, head:] = grad_key[rows:], grad_value[rows:]


def shard_row(step, count):
    return lax.rem(lax.axis_index("yh") + count - step, count)


def relayout_kernel(y_half, tokens_ref, out_ref):
    members, _, columns = out_ref.shape
    quarter = columns // (2 * y_half)
    core = lax.axis_index("core")
    for member in range(members):
        x_hi, y_lo, z_lo = member // 4, member // 2 % 2, member % 2
        for half in range(2):
            for step in range(y_half):
                shard = (x_hi * y_half + shard_row(step, y_half)) * 2 + y_lo
                start = (shard * 4 + z_lo * 2 + (core ^ half)) * quarter
                target = (half * y_half + step) * quarter
                out_ref[member, :, target : target + quarter] = tokens_ref[
                    :, pl.ds(pl.multiple_of(start, quarter), quarter)
                ]


def project_kernel(x_ref, near_ref, far_ref, out_ref):
    depth = near_ref.shape[0]
    total = dot_f32(x_ref[:, :depth], near_ref[...], 1, 0)
    total = total + dot_f32(x_ref[:, depth:], far_ref[...], 1, 0)
    out_ref[...] = total.astype(low)


def weight_kernel(y_half, x_ref, grad_ref, out_ref):
    total = dot_f32(x_ref[...], grad_ref[...], 0, 0).astype(out_ref.dtype)
    quarter = total.shape[0] // y_half
    for step in range(y_half):
        out_ref[shard_row(step, y_half)] = total[step * quarter : (step + 1) * quarter]


def in_vmem(count):
    return [pl.BlockSpec(memory_space=pltpu.VMEM)] * count


def on_device(tokens, qkv_weight, out_grad):
    y_half, z_count = lax.axis_size("yh"), lax.axis_size(z_axes)
    ctx_count = z_count * 4
    row_count, model, width = tokens.shape[1], tokens.shape[2], qkv_weight.shape[1]
    shard, head = qkv_weight.shape[0], qkv_weight.shape[1] // 3
    quarter, depth, group_rows = shard // 4, model // 16, 8 * row_count
    cotangent = out_grad[0]

    at = (lax.axis_index("zl") * 2 + lax.axis_index("core")) * quarter
    own_weight = lax.dynamic_slice_in_dim(qkv_weight, at, quarter)
    steps = [own_weight]
    for step in range(1, y_half):
        ring = [(i, (i + step) % y_half) for i in range(y_half)]
        steps.append(lax.ppermute(own_weight, "yh", ring))
    near = jnp.concatenate(steps)
    split = pl.pallas_call(
        functools.partial(relayout_kernel, y_half),
        in_specs=in_vmem(1),
        out_specs=in_vmem(1)[0],
        out_shape=jax.ShapeDtypeStruct((8, row_count, 2 * depth), low),
        compiler_params=vmem,
        name="token_columns",
    )(tokens[0])
    split, near = lax.optimization_barrier((split, near))
    far = swap(near, "core")
    columns = exchange(split, group_axes).reshape(group_rows, 2 * depth)
    parts = pl.pallas_call(
        project_kernel,
        in_specs=in_vmem(3),
        out_specs=in_vmem(1)[0],
        out_shape=jax.ShapeDtypeStruct((group_rows, width), low),
        compiler_params=vmem,
        name="partial_projection",
    )(columns, near, far)
    parts = exchange(parts.reshape(8, row_count, width), group_axes)
    qkv = jnp.sum(parts.astype(jnp.float32), axis=0).astype(low)
    queries, own_pairs = qkv[:, :head], qkv[:, head:]
    pair_pieces = gather_x(own_pairs)
    pair_pieces = pair_pieces + tuple(swap(p, "core") for p in pair_pieces)
    query_pieces = gather_x(jnp.concatenate([queries, cotangent], axis=1))

    attn_rows, stats, grad_query = pl.pallas_call(
        functools.partial(forward_kernel, z_count),
        in_specs=in_vmem(6),
        out_specs=in_vmem(3),
        out_shape=[
            jax.ShapeDtypeStruct((row_count, head), low),
            jax.ShapeDtypeStruct((2, row_count), jnp.float32),
            jax.ShapeDtypeStruct((row_count, head), low),
        ],
        scratch_shapes=[pltpu.VMEM((4, row_count, z_count * row_count), jnp.float32)],
        compiler_params=vmem,
        name="attention_rows",
    )(queries, *pair_pieces, cotangent)

    stats_all = spread(stats, z_axes + ("xl",), 2 * z_count)

    own_part, other_part = pl.pallas_call(
        functools.partial(backward_kernel, z_count),
        in_specs=in_vmem(5),
        out_specs=in_vmem(2),
        out_shape=[jax.ShapeDtypeStruct((row_count, 2 * head), jnp.float32)] * 2,
        compiler_params=vmem,
        name="attention_columns",
    )(own_pairs, pair_pieces[2], *query_pieces, stats_all)
    grad_pairs = (own_part + swap(other_part, "core")).astype(low)

    grad_all = spread(jnp.concatenate([grad_query, grad_pairs], axis=1), group_axes, 8)
    grad_all = grad_all.reshape(group_rows, width)

    def weight_half(half, dtype):
        return pl.pallas_call(
            functools.partial(weight_kernel, y_half),
            grid=(1,),
            in_specs=[
                pl.BlockSpec((group_rows, depth), lambda i: (0, half)),
                pl.BlockSpec((group_rows, width), lambda i: (0, 0)),
            ],
            out_specs=pl.BlockSpec((y_half, quarter, width), lambda i: (0, 0, 0)),
            out_shape=jax.ShapeDtypeStruct((y_half, quarter, width), dtype),
            compiler_params=vmem,
            name="weight_gradient",
        )(columns, grad_all)

    sent = swap(weight_half(1, low), "core")
    summed = (weight_half(0, jnp.float32) + sent.astype(jnp.float32)).astype(low)
    pieces = exchange(summed.reshape(8 * y_half, -1, width), ("yh", "zh", "xl"))
    own_piece = jnp.sum(pieces.astype(jnp.float32), axis=0).astype(low)
    on_core = spread(own_piece, z_axes + ("xl",), 2 * z_count)
    on_core = on_core.reshape((z_count // 2, 2, 2) + own_piece.shape).transpose(1, 0, 2, 3, 4)
    across = swap(on_core, "core")
    first = lax.axis_index("core") == 0
    total = jnp.stack([jnp.where(first, on_core, across), jnp.where(first, across, on_core)], axis=1)
    return (attn_rows[None], total.reshape(shard, width))


def solution(mesh):
    grid = Mesh(mesh.devices.reshape(2, 4, 2, 4, 2, 2, 2), ("xh", "yh", "yl") + ctx_axes)
    rows, weights = P(("xh", "yh", "yl"), ctx_axes, None), P(("xh", "yh", "yl"), None)
    return jax.shard_map(
        on_device,
        mesh=grid,
        in_specs=(rows, weights, rows),
        out_specs=(rows, weights),
        check_vma=False,
    )
```

```python
import functools
import math

import jax
import jax.numpy as jnp
from jax import lax
from jax.experimental import pallas as pl
from jax.experimental.pallas import tpu as pltpu
from jax.sharding import Mesh, PartitionSpec as P

z_weight = 0.001
masked_fill = -1e30
low = jnp.bfloat16
z_axes = ("zh", "zl")
ctx_axes = z_axes + ("xl", "core")
group_axes = ("xh", "yl", "zl")
vmem = pltpu.CompilerParams(vmem_limit_bytes=32 * 1024 * 1024)


def dot_f32(left, right, left_dim, right_dim):
    return lax.dot_general(
        left, right, (((left_dim,), (right_dim,)), ((), ())), preferred_element_type=jnp.float32
    )


def exchange(blocks, axes):
    return lax.all_to_all(blocks, axes, split_axis=0, concat_axis=0, tiled=True)


def spread(block, axes, count):
    return exchange(jnp.broadcast_to(block[None], (count,) + block.shape), axes)


def swap(block, axis):
    return lax.ppermute(block, axis, ((0, 1), (1, 0)))


def gather_z(block):
    return spread(block, z_axes, lax.axis_size(z_axes)).reshape(-1, block.shape[1])


def positions(device, inside, half_rows, ctx_count):
    block = jnp.where(inside < half_rows, device, 2 * ctx_count - 1 - device)
    return block * half_rows + inside % half_rows


def piece_device(piece, z):
    return z * 4 + (lax.axis_index("xl") ^ (piece & 1)) * 2 + (lax.axis_index("core") ^ (piece >> 1))


def forward_kernel(
    z_count, q_ref, kv0, kv1, kv2, kv3, cot_ref, attn_ref, stats_ref, dq_ref, held
):
    pieces = (kv0, kv1, kv2, kv3)
    rows, head = q_ref.shape
    half_rows, ctx_count = rows // 2, 4 * z_count
    scale = 1.0 / math.sqrt(head)
    own = piece_device(0, lax.axis_index(z_axes))
    down = lax.broadcasted_iota(jnp.int32, (rows, rows), 0)
    across = lax.broadcasted_iota(jnp.int32, (rows, rows), 1)
    own_positions = positions(own, down, half_rows, ctx_count)
    queries, cotangent = q_ref[...], cot_ref[...]
    top = None
    for piece, kv in enumerate(pieces):
        raw = dot_f32(queries, kv[:, :head], 1, 1) * scale
        for z in range(z_count):
            device = piece_device(piece, z)
            allowed = positions(device, across, half_rows, ctx_count) <= own_positions
            tile = jnp.where(allowed, raw[:, z * rows : (z + 1) * rows], masked_fill)
            held[piece, :, z * rows : (z + 1) * rows] = tile
            top = tile if top is None else jnp.maximum(top, tile)
    row_top = jnp.max(top, axis=1, keepdims=True)
    total = jnp.zeros((rows, rows), jnp.float32)
    for piece in range(4):
        weights = jnp.exp(held[piece] - row_top)
        held[piece] = weights
        for z in range(z_count):
            total = total + weights[:, z * rows : (z + 1) * rows]
    row_sum = jnp.sum(total, axis=1, keepdims=True)
    inverse = 1.0 / row_sum
    log_total = row_top + jnp.log(row_sum)
    attn = jnp.zeros((rows, head), jnp.float32)
    for piece, kv in enumerate(pieces):
        attn = attn + dot_f32((held[piece] * inverse).astype(low), kv[:, head:], 1, 0)
    attn_low = attn.astype(low)
    attn_ref[...] = attn_low
    delta = jnp.sum(
        cotangent.astype(jnp.float32) * attn_low.astype(jnp.float32), axis=1, keepdims=True
    )
    shift = 2.0 * z_weight * log_total - delta
    stats_ref[0:1, :] = jnp.transpose(jnp.broadcast_to(log_total, (rows, rows)))[0:1, :]
    stats_ref[1:2, :] = jnp.transpose(jnp.broadcast_to(shift, (rows, rows)))[0:1, :]
    grad = jnp.zeros((rows, head), jnp.float32)
    for piece, kv in enumerate(pieces):
        dprob = dot_f32(cotangent, kv[:, head:], 1, 1)
        dscore = held[piece] * inverse * (dprob + shift)
        grad = grad + dot_f32(dscore.astype(low), kv[:, :head], 1, 0)
    dq_ref[...] = (grad * scale).astype(low)


def backward_kernel(z_count, kv_ref, across_ref, q0, q1, cot_ref, stats_ref, own_ref, other_ref):
    rows, head = kv_ref.shape[0], kv_ref.shape[1] // 2
    half_rows, ctx_count = rows // 2, 4 * z_count
    scale = 1.0 / math.sqrt(head)
    z_own = lax.axis_index(z_axes)
    down = lax.broadcasted_iota(jnp.int32, (rows, rows), 0)
    across = lax.broadcasted_iota(jnp.int32, (rows, rows), 1)
    key_positions = jnp.concatenate(
        [
            positions(piece_device(0, z_own), down, half_rows, ctx_count),
            positions(piece_device(2, z_own), down, half_rows, ctx_count),
        ],
        axis=0,
    )
    pairs = jnp.concatenate(
        [kv_ref[...], across_ref[pl.ds(pl.multiple_of(z_own * rows, rows), rows), :]], axis=0
    )
    keys, values = pairs[:, :head], pairs[:, head:]
    grad_key = jnp.zeros((2 * rows, head), jnp.float32)
    grad_value = jnp.zeros((2 * rows, head), jnp.float32)
    for piece, queries_ref in enumerate((q0, q1)):
        slot = lax.axis_index("xl") ^ piece
        queries = queries_ref[...]
        cotangent = jnp.concatenate(
            [cot_ref[2 * z + slot, :, :head] for z in range(z_count)], axis=0
        )
        scores = dot_f32(keys, queries, 1, 1) * scale
        dprob = dot_f32(values, cotangent, 1, 1)
        probs, dscores = [], []
        for z in range(z_count):
            span = slice(z * rows, (z + 1) * rows)
            stats = stats_ref[2 * z + slot]
            row_positions = positions(piece_device(piece, z), across, half_rows, ctx_count)
            allowed = key_positions <= jnp.concatenate([row_positions, row_positions], axis=0)
            masked = jnp.where(allowed, scores[:, span], masked_fill)
            prob = jnp.exp(masked - stats[0:1, :])
            probs.append(prob.astype(low))
            dscores.append((prob * (dprob[:, span] + stats[1:2, :])).astype(low))
        grad_value = grad_value + dot_f32(jnp.concatenate(probs, axis=1), cotangent, 1, 0)
        grad_key = grad_key + dot_f32(jnp.concatenate(dscores, axis=1), queries, 1, 0)
    grad_key = grad_key * scale
    own_ref[:, :head], own_ref[:, head:] = grad_key[:rows], grad_value[:rows]
    other_ref[:, :head], other_ref[:, head:] = grad_key[rows:], grad_value[rows:]


def relayout_kernel(y_half, tokens_ref, out_ref):
    members, _, columns = out_ref.shape
    span = columns // y_half
    for member in range(members):
        x_hi, y_lo, z_lo = member // 4, member // 2 % 2, member % 2
        for y_hi in range(y_half):
            start = (((x_hi * y_half + y_hi) * 2 + y_lo) * 2 + z_lo) * span
            out_ref[member, :, y_hi * span : (y_hi + 1) * span] = tokens_ref[:, start : start + span]


def project_kernel(x_ref, weight_ref, out_ref):
    out_ref[...] = dot_f32(x_ref[...], weight_ref[...], 1, 0).astype(low)


def weight_kernel(y_half, half, x_ref, grad_ref, out_ref):
    quarter = x_ref.shape[1] // (2 * y_half)
    core = lax.axis_index("core") ^ half
    columns = []
    for y_hi in range(y_half):
        start = pl.multiple_of((y_hi * 2 + core) * quarter, quarter)
        columns.append(x_ref[:, pl.ds(start, quarter)])
    total = dot_f32(jnp.concatenate(columns, axis=1), grad_ref[...], 0, 0)
    out_ref[...] = total.astype(out_ref.dtype)


def in_vmem(count):
    return [pl.BlockSpec(memory_space=pltpu.VMEM)] * count


def on_device(tokens, qkv_weight, out_grad):
    y_half, z_count = lax.axis_size("yh"), lax.axis_size(z_axes)
    ctx_count = z_count * 4
    row_count, model, width = tokens.shape[1], tokens.shape[2], qkv_weight.shape[1]
    shard, head = qkv_weight.shape[0], qkv_weight.shape[1] // 3
    quarter, depth, group_rows = shard // 4, model // 16, 8 * row_count
    cotangent = out_grad[0]

    split = pl.pallas_call(
        functools.partial(relayout_kernel, y_half),
        in_specs=in_vmem(1),
        out_specs=in_vmem(1)[0],
        out_shape=jax.ShapeDtypeStruct((8, row_count, 2 * depth), low),
        compiler_params=vmem,
        name="token_columns",
    )(tokens[0])
    columns = exchange(split, group_axes).reshape(group_rows, 2 * depth)
    at = (lax.axis_index("zl") * 2 + lax.axis_index("core")) * quarter
    own_weight = lax.dynamic_slice_in_dim(qkv_weight, at, quarter)
    weight = lax.all_gather(own_weight, ("yh", "core"), axis=0, tiled=True)
    parts = pl.pallas_call(
        project_kernel,
        in_specs=in_vmem(2),
        out_specs=in_vmem(1)[0],
        out_shape=jax.ShapeDtypeStruct((group_rows, width), low),
        compiler_params=vmem,
        name="partial_projection",
    )(columns, weight)
    parts = exchange(parts.reshape(8, row_count, width), group_axes)
    qkv = jnp.sum(parts.astype(jnp.float32), axis=0).astype(low)
    queries, own_pairs = qkv[:, :head], qkv[:, head:]
    cotangent_all = lax.all_gather(
        jnp.concatenate([cotangent, cotangent], axis=1), z_axes + ("xl",), axis=0, tiled=False
    )
    along_z, cotangent_all = lax.optimization_barrier((gather_z(own_pairs), cotangent_all))
    pair_pieces = (along_z, swap(along_z, "xl"))
    pair_pieces = pair_pieces + tuple(swap(p, "core") for p in pair_pieces)
    queries_z = gather_z(queries)
    query_pieces = (queries_z, swap(queries_z, "xl"))

    attn_rows, stats, grad_query = pl.pallas_call(
        functools.partial(forward_kernel, z_count),
        in_specs=in_vmem(6),
        out_specs=in_vmem(3),
        out_shape=[
            jax.ShapeDtypeStruct((row_count, head), low),
            jax.ShapeDtypeStruct((2, row_count), jnp.float32),
            jax.ShapeDtypeStruct((row_count, head), low),
        ],
        scratch_shapes=[pltpu.VMEM((4, row_count, z_count * row_count), jnp.float32)],
        compiler_params=vmem,
        name="attention_rows",
    )(queries, *pair_pieces, cotangent)

    stats_all = spread(stats, z_axes + ("xl",), 2 * z_count)

    own_part, other_part = pl.pallas_call(
        functools.partial(backward_kernel, z_count),
        in_specs=in_vmem(6),
        out_specs=in_vmem(2),
        out_shape=[jax.ShapeDtypeStruct((row_count, 2 * head), jnp.float32)] * 2,
        compiler_params=vmem,
        name="attention_columns",
    )(own_pairs, pair_pieces[2], *query_pieces, cotangent_all, stats_all)
    grad_pairs = (own_part + swap(other_part, "core")).astype(low)

    grad_all = spread(jnp.concatenate([grad_query, grad_pairs], axis=1), group_axes, 8)
    grad_all = grad_all.reshape(group_rows, width)

    def weight_half(half, dtype):
        return pl.pallas_call(
            functools.partial(weight_kernel, y_half, half),
            in_specs=in_vmem(2),
            out_specs=in_vmem(1)[0],
            out_shape=jax.ShapeDtypeStruct((depth, width), dtype),
            compiler_params=vmem,
            name="weight_gradient",
        )(columns, grad_all)

    sent = swap(weight_half(1, low), "core")
    summed = (weight_half(0, jnp.float32) + sent.astype(jnp.float32)).astype(low)
    pieces = exchange(summed.reshape(8 * y_half, -1, width), ("yh", "zh", "xl"))
    own_piece = jnp.sum(pieces.astype(jnp.float32), axis=0).astype(low)
    on_core = spread(own_piece, z_axes + ("xl",), 2 * z_count)
    on_core = on_core.reshape((z_count // 2, 2, 2) + own_piece.shape).transpose(1, 0, 2, 3, 4)
    across = swap(on_core, "core")
    first = lax.axis_index("core") == 0
    total = jnp.stack([jnp.where(first, on_core, across), jnp.where(first, across, on_core)], axis=1)
    return (attn_rows[None], total.reshape(shard, width))


def solution(mesh):
    grid = Mesh(mesh.devices.reshape(2, 4, 2, 4, 2, 2, 2), ("xh", "yh", "yl") + ctx_axes)
    rows, weights = P(("xh", "yh", "yl"), ctx_axes, None), P(("xh", "yh", "yl"), None)
    return jax.shard_map(
        on_device,
        mesh=grid,
        in_specs=(rows, weights, rows),
        out_specs=(rows, weights),
        check_vma=False,
    )
```

```python
import functools
import math

import jax
import jax.numpy as jnp
from jax import lax
from jax.experimental import pallas as pl
from jax.experimental.pallas import tpu as pltpu
from jax.sharding import Mesh, PartitionSpec as P

z_weight = 0.001
masked_fill = -1e30
low = jnp.bfloat16
z_axes = ("zh", "zl")
ctx_axes = z_axes + ("xl", "core")
group_axes = ("xh", "zl")
vmem = pltpu.CompilerParams(vmem_limit_bytes=32 * 1024 * 1024)


def dot_f32(left, right, left_dim, right_dim):
    return lax.dot_general(
        left, right, (((left_dim,), (right_dim,)), ((), ())), preferred_element_type=jnp.float32
    )


def exchange(blocks, axes):
    return lax.all_to_all(blocks, axes, split_axis=0, concat_axis=0, tiled=True)


def spread(block, axes, count):
    return exchange(jnp.broadcast_to(block[None], (count,) + block.shape), axes)


def swap(block, axis):
    return lax.ppermute(block, axis, ((0, 1), (1, 0)))


def gather_x(block):
    along_z = spread(block, z_axes, lax.axis_size(z_axes)).reshape(-1, block.shape[1])
    return along_z, swap(along_z, "xl")


def positions(device, inside, half_rows, ctx_count):
    block = jnp.where(inside < half_rows, device, 2 * ctx_count - 1 - device)
    return block * half_rows + inside % half_rows


def piece_device(piece, z):
    return z * 4 + (lax.axis_index("xl") ^ (piece & 1)) * 2 + (lax.axis_index("core") ^ (piece >> 1))


def forward_kernel(
    z_count, q_ref, kv0, kv1, kv2, kv3, cot_ref, attn_ref, stats_ref, dq_ref, held
):
    pieces = (kv0, kv1, kv2, kv3)
    rows, head = q_ref.shape
    half_rows, ctx_count = rows // 2, 4 * z_count
    scale = 1.0 / math.sqrt(head)
    own = piece_device(0, lax.axis_index(z_axes))
    down = lax.broadcasted_iota(jnp.int32, (rows, rows), 0)
    across = lax.broadcasted_iota(jnp.int32, (rows, rows), 1)
    own_positions = positions(own, down, half_rows, ctx_count)
    queries, cotangent = q_ref[...], cot_ref[...]
    top = None
    for piece, kv in enumerate(pieces):
        raw = dot_f32(queries, kv[:, :head], 1, 1) * scale
        for z in range(z_count):
            device = piece_device(piece, z)
            allowed = positions(device, across, half_rows, ctx_count) <= own_positions
            tile = jnp.where(allowed, raw[:, z * rows : (z + 1) * rows], masked_fill)
            held[piece, :, z * rows : (z + 1) * rows] = tile
            top = tile if top is None else jnp.maximum(top, tile)
    row_top = jnp.max(top, axis=1, keepdims=True)
    total = jnp.zeros((rows, rows), jnp.float32)
    for piece in range(4):
        weights = jnp.exp(held[piece] - row_top)
        held[piece] = weights
        for z in range(z_count):
            total = total + weights[:, z * rows : (z + 1) * rows]
    row_sum = jnp.sum(total, axis=1, keepdims=True)
    inverse = 1.0 / row_sum
    log_total = row_top + jnp.log(row_sum)
    attn = jnp.zeros((rows, head), jnp.float32)
    for piece, kv in enumerate(pieces):
        attn = attn + dot_f32((held[piece] * inverse).astype(low), kv[:, head:], 1, 0)
    attn_low = attn.astype(low)
    attn_ref[...] = attn_low
    delta = jnp.sum(
        cotangent.astype(jnp.float32) * attn_low.astype(jnp.float32), axis=1, keepdims=True
    )
    shift = 2.0 * z_weight * log_total - delta
    stats_ref[0:1, :] = jnp.transpose(jnp.broadcast_to(log_total, (rows, rows)))[0:1, :]
    stats_ref[1:2, :] = jnp.transpose(jnp.broadcast_to(shift, (rows, rows)))[0:1, :]
    grad = jnp.zeros((rows, head), jnp.float32)
    for piece, kv in enumerate(pieces):
        dprob = dot_f32(cotangent, kv[:, head:], 1, 1)
        dscore = held[piece] * inverse * (dprob + shift)
        grad = grad + dot_f32(dscore.astype(low), kv[:, :head], 1, 0)
    dq_ref[...] = (grad * scale).astype(low)


def backward_kernel(z_count, kv_ref, across_ref, qc0, qc1, stats_ref, own_ref, other_ref):
    rows, head = kv_ref.shape[0], kv_ref.shape[1] // 2
    half_rows, ctx_count = rows // 2, 4 * z_count
    scale = 1.0 / math.sqrt(head)
    z_own = lax.axis_index(z_axes)
    down = lax.broadcasted_iota(jnp.int32, (rows, rows), 0)
    across = lax.broadcasted_iota(jnp.int32, (rows, rows), 1)
    key_positions = jnp.concatenate(
        [
            positions(piece_device(0, z_own), down, half_rows, ctx_count),
            positions(piece_device(2, z_own), down, half_rows, ctx_count),
        ],
        axis=0,
    )
    pairs = jnp.concatenate(
        [kv_ref[...], across_ref[pl.ds(pl.multiple_of(z_own * rows, rows), rows), :]], axis=0
    )
    keys, values = pairs[:, :head], pairs[:, head:]
    grad_key = jnp.zeros((2 * rows, head), jnp.float32)
    grad_value = jnp.zeros((2 * rows, head), jnp.float32)
    for piece, both in enumerate((qc0, qc1)):
        slot = lax.axis_index("xl") ^ piece
        queries, cotangent = both[:, :head], both[:, head:]
        scores = dot_f32(keys, queries, 1, 1) * scale
        dprob = dot_f32(values, cotangent, 1, 1)
        probs, dscores = [], []
        for z in range(z_count):
            span = slice(z * rows, (z + 1) * rows)
            stats = stats_ref[2 * z + slot]
            row_positions = positions(piece_device(piece, z), across, half_rows, ctx_count)
            allowed = key_positions <= jnp.concatenate([row_positions, row_positions], axis=0)
            masked = jnp.where(allowed, scores[:, span], masked_fill)
            prob = jnp.exp(masked - stats[0:1, :])
            probs.append(prob.astype(low))
            dscores.append((prob * (dprob[:, span] + stats[1:2, :])).astype(low))
        grad_value = grad_value + dot_f32(jnp.concatenate(probs, axis=1), cotangent, 1, 0)
        grad_key = grad_key + dot_f32(jnp.concatenate(dscores, axis=1), queries, 1, 0)
    grad_key = grad_key * scale
    own_ref[:, :head], own_ref[:, head:] = grad_key[:rows], grad_value[:rows]
    other_ref[:, :head], other_ref[:, head:] = grad_key[rows:], grad_value[rows:]


def relayout_kernel(y_count, tokens_ref, out_ref):
    members, _, columns = out_ref.shape
    quarter = columns // (2 * y_count)
    core = lax.axis_index("core")
    for member in range(members):
        x_hi, z_lo = member // 2, member % 2
        for half in range(2):
            for y in range(y_count):
                start = ((x_hi * y_count + y) * 4 + z_lo * 2 + (core ^ half)) * quarter
                target = (half * y_count + y) * quarter
                out_ref[member, :, target : target + quarter] = tokens_ref[
                    :, pl.ds(pl.multiple_of(start, quarter), quarter)
                ]


def project_kernel(x_ref, near_ref, far_ref, out_ref):
    depth = near_ref.shape[0]
    total = dot_f32(x_ref[:, :depth], near_ref[...], 1, 0)
    total = total + dot_f32(x_ref[:, depth:], far_ref[...], 1, 0)
    out_ref[...] = total.astype(low)


def weight_kernel(x_ref, grad_ref, out_ref):
    out_ref[...] = dot_f32(x_ref[...], grad_ref[...], 0, 0).astype(out_ref.dtype)


def in_vmem(count):
    return [pl.BlockSpec(memory_space=pltpu.VMEM)] * count


def on_device(tokens, qkv_weight, out_grad):
    y_count, z_count = lax.axis_size("y"), lax.axis_size(z_axes)
    ctx_count = z_count * 4
    row_count, model, width = tokens.shape[1], tokens.shape[2], qkv_weight.shape[1]
    shard, head = qkv_weight.shape[0], qkv_weight.shape[1] // 3
    quarter, depth, group_rows = shard // 4, model // 8, 4 * row_count
    cotangent = out_grad[0]

    at = (lax.axis_index("zl") * 2 + lax.axis_index("core")) * quarter
    own_weight = lax.dynamic_slice_in_dim(qkv_weight, at, quarter)
    near = lax.all_gather(own_weight, "y", axis=0, tiled=True)
    far = swap(near, "core")
    split = pl.pallas_call(
        functools.partial(relayout_kernel, y_count),
        in_specs=in_vmem(1),
        out_specs=in_vmem(1)[0],
        out_shape=jax.ShapeDtypeStruct((4, row_count, 2 * depth), low),
        compiler_params=vmem,
        name="token_columns",
    )(tokens[0])
    columns = exchange(split, group_axes).reshape(group_rows, 2 * depth)
    parts = pl.pallas_call(
        project_kernel,
        in_specs=in_vmem(3),
        out_specs=in_vmem(1)[0],
        out_shape=jax.ShapeDtypeStruct((group_rows, width), low),
        compiler_params=vmem,
        name="partial_projection",
    )(columns, near, far)
    parts = exchange(parts.reshape(4, row_count, width), group_axes)
    qkv = jnp.sum(parts.astype(jnp.float32), axis=0).astype(low)
    queries, own_pairs = qkv[:, :head], qkv[:, head:]
    pair_pieces = gather_x(own_pairs)
    pair_pieces = pair_pieces + tuple(swap(p, "core") for p in pair_pieces)
    query_pieces = gather_x(jnp.concatenate([queries, cotangent], axis=1))

    attn_rows, stats, grad_query = pl.pallas_call(
        functools.partial(forward_kernel, z_count),
        in_specs=in_vmem(6),
        out_specs=in_vmem(3),
        out_shape=[
            jax.ShapeDtypeStruct((row_count, head), low),
            jax.ShapeDtypeStruct((2, row_count), jnp.float32),
            jax.ShapeDtypeStruct((row_count, head), low),
        ],
        scratch_shapes=[pltpu.VMEM((4, row_count, z_count * row_count), jnp.float32)],
        compiler_params=vmem,
        name="attention_rows",
    )(queries, *pair_pieces, cotangent)

    stats_all = spread(stats, z_axes + ("xl",), 2 * z_count)

    own_part, other_part = pl.pallas_call(
        functools.partial(backward_kernel, z_count),
        in_specs=in_vmem(5),
        out_specs=in_vmem(2),
        out_shape=[jax.ShapeDtypeStruct((row_count, 2 * head), jnp.float32)] * 2,
        compiler_params=vmem,
        name="attention_columns",
    )(own_pairs, pair_pieces[2], *query_pieces, stats_all)
    grad_pairs = (own_part + swap(other_part, "core")).astype(low)

    grad_all = spread(jnp.concatenate([grad_query, grad_pairs], axis=1), group_axes, 4)
    grad_all = grad_all.reshape(group_rows, width)

    def weight_half(half, dtype):
        return pl.pallas_call(
            weight_kernel,
            grid=(1,),
            in_specs=[
                pl.BlockSpec((group_rows, depth), lambda i: (0, half)),
                pl.BlockSpec((group_rows, width), lambda i: (0, 0)),
            ],
            out_specs=pl.BlockSpec((depth, width), lambda i: (0, 0)),
            out_shape=jax.ShapeDtypeStruct((depth, width), dtype),
            compiler_params=vmem,
            name="weight_gradient",
        )(columns, grad_all)

    sent = swap(weight_half(1, low), "core")
    summed = (weight_half(0, jnp.float32) + sent.astype(jnp.float32)).astype(low)
    pieces = exchange(summed.reshape(z_count * y_count, -1, width), ("y", "zh", "xl"))
    own_piece = jnp.sum(pieces.astype(jnp.float32), axis=0).astype(low)
    on_core = spread(own_piece, z_axes + ("xl",), 2 * z_count)
    on_core = on_core.reshape((z_count // 2, 2, 2) + own_piece.shape).transpose(1, 0, 2, 3, 4)
    across = swap(on_core, "core")
    first = lax.axis_index("core") == 0
    total = jnp.stack([jnp.where(first, on_core, across), jnp.where(first, across, on_core)], axis=1)
    return (attn_rows[None], total.reshape(shard, width))


def solution(mesh):
    grid = Mesh(mesh.devices.reshape(2, 8, 4, 2, 2, 2), ("xh", "y") + ctx_axes)
    rows, weights = P(("xh", "y"), ctx_axes, None), P(("xh", "y"), None)
    return jax.shard_map(
        on_device,
        mesh=grid,
        in_specs=(rows, weights, rows),
        out_specs=(rows, weights),
        check_vma=False,
    )
```

```python
import functools
import math

import jax
import jax.numpy as jnp
from jax import lax
from jax.experimental import pallas as pl
from jax.experimental.pallas import tpu as pltpu
from jax.sharding import Mesh, PartitionSpec as P

z_weight = 0.001
masked_fill = -1e30
low = jnp.bfloat16
z_axes = ("zh", "zl")
ctx_axes = z_axes + ("xl", "core")
group_axes = ("xh", "zl")
vmem = pltpu.CompilerParams(vmem_limit_bytes=32 * 1024 * 1024)


def dot_f32(left, right, left_dim, right_dim):
    return lax.dot_general(
        left, right, (((left_dim,), (right_dim,)), ((), ())), preferred_element_type=jnp.float32
    )


def exchange(blocks, axes):
    return lax.all_to_all(blocks, axes, split_axis=0, concat_axis=0, tiled=True)


def spread(block, axes, count):
    return exchange(jnp.broadcast_to(block[None], (count,) + block.shape), axes)


def swap(block, axis):
    return lax.ppermute(block, axis, ((0, 1), (1, 0)))


def positions(device, inside, half_rows, ctx_count):
    block = jnp.where(inside < half_rows, device, 2 * ctx_count - 1 - device)
    return block * half_rows + inside % half_rows


def piece_device(piece, z):
    return z * 4 + (lax.axis_index("xl") ^ (piece & 1)) * 2 + (lax.axis_index("core") ^ (piece >> 1))


def row_scores(z_count, q_ref, kv_refs):
    rows, head = q_ref.shape
    half_rows, ctx_count = rows // 2, 4 * z_count
    scale = 1.0 / math.sqrt(head)
    own = piece_device(0, lax.axis_index(z_axes))
    down = lax.broadcasted_iota(jnp.int32, (rows, rows), 0)
    across = lax.broadcasted_iota(jnp.int32, (rows, rows), 1)
    own_positions = positions(own, down, half_rows, ctx_count)
    for piece, kv in enumerate(kv_refs):
        raw = dot_f32(q_ref[...], kv[:, :head], 1, 1) * scale
        tiles = []
        for z in range(z_count):
            device = piece_device(piece, z)
            allowed = positions(device, across, half_rows, ctx_count) <= own_positions
            tiles.append(jnp.where(allowed, raw[:, z * rows : (z + 1) * rows], masked_fill))
        yield tiles


def forward_kernel(
    z_count, q_ref, kv0, kv1, kv2, kv3, cot_ref, attn_ref, stats_ref, columns_ref, held
):
    pieces = (kv0, kv1, kv2, kv3)
    rows, head = q_ref.shape
    top = None
    for piece, tiles in enumerate(row_scores(z_count, q_ref, pieces)):
        for z, tile in enumerate(tiles):
            held[piece, :, z * rows : (z + 1) * rows] = tile
            top = tile if top is None else jnp.maximum(top, tile)
    row_top = jnp.max(top, axis=1, keepdims=True)
    total = jnp.zeros((rows, rows), jnp.float32)
    for piece in range(4):
        weights = jnp.exp(held[piece] - row_top)
        held[piece] = weights
        for z in range(z_count):
            total = total + weights[:, z * rows : (z + 1) * rows]
    row_sum = jnp.sum(total, axis=1, keepdims=True)
    inverse = 1.0 / row_sum
    log_total = row_top + jnp.log(row_sum)
    attn = jnp.zeros((rows, head), jnp.float32)
    for piece, kv in enumerate(pieces):
        attn = attn + dot_f32((held[piece] * inverse).astype(low), kv[:, head:], 1, 0)
    attn_low = attn.astype(low)
    attn_ref[...] = attn_low
    delta = jnp.sum(
        cot_ref[...].astype(jnp.float32) * attn_low.astype(jnp.float32), axis=1, keepdims=True
    )
    shift = 2.0 * z_weight * log_total - delta
    for place, column in enumerate((log_total, shift)):
        wide = jnp.broadcast_to(column, (rows, rows))
        columns_ref[place] = wide
        line = jnp.transpose(wide)[0:1, :]
        for copy in range(stats_ref.shape[0]):
            stats_ref[copy, place : place + 1, :] = line


def query_kernel(z_count, q_ref, kv0, kv1, kv2, kv3, cot_ref, columns_ref, dq_ref):
    pieces = (kv0, kv1, kv2, kv3)
    rows, head = q_ref.shape
    log_total, shift = columns_ref[0], columns_ref[1]
    grad = jnp.zeros((rows, head), jnp.float32)
    for kv, tiles in zip(pieces, row_scores(z_count, q_ref, pieces)):
        dprob = dot_f32(cot_ref[...], kv[:, head:], 1, 1)
        dscores = []
        for z, tile in enumerate(tiles):
            prob = jnp.exp(tile - log_total)
            dscores.append((prob * (dprob[:, z * rows : (z + 1) * rows] + shift)).astype(low))
        grad = grad + dot_f32(jnp.concatenate(dscores, axis=1), kv[:, :head], 1, 0)
    dq_ref[...] = (grad * (1.0 / math.sqrt(head))).astype(low)


def backward_kernel(z_count, kv_ref, across_ref, q0, q1, cot0, cot1, stats_ref, own_ref, other_ref):
    rows, head = kv_ref.shape[0], kv_ref.shape[1] // 2
    half_rows, ctx_count = rows // 2, 4 * z_count
    scale = 1.0 / math.sqrt(head)
    z_own = lax.axis_index(z_axes)
    down = lax.broadcasted_iota(jnp.int32, (rows, rows), 0)
    across = lax.broadcasted_iota(jnp.int32, (rows, rows), 1)
    key_positions = jnp.concatenate(
        [
            positions(piece_device(0, z_own), down, half_rows, ctx_count),
            positions(piece_device(2, z_own), down, half_rows, ctx_count),
        ],
        axis=0,
    )
    pairs = jnp.concatenate(
        [kv_ref[...], across_ref[pl.ds(pl.multiple_of(z_own * rows, rows), rows), :]], axis=0
    )
    keys, values = pairs[:, :head], pairs[:, head:]
    grad_key = jnp.zeros((2 * rows, head), jnp.float32)
    grad_value = jnp.zeros((2 * rows, head), jnp.float32)
    for piece, (q_ref, cot_ref) in enumerate(((q0, cot0), (q1, cot1))):
        slot = lax.axis_index("xl") ^ piece
        queries, cotangent = q_ref[...], cot_ref[...]
        scores = dot_f32(keys, queries, 1, 1) * scale
        dprob = dot_f32(values, cotangent, 1, 1)
        probs, dscores = [], []
        for z in range(z_count):
            span = slice(z * rows, (z + 1) * rows)
            stats = stats_ref[2 * z + slot]
            row_positions = positions(piece_device(piece, z), across, half_rows, ctx_count)
            allowed = key_positions <= jnp.concatenate([row_positions, row_positions], axis=0)
            masked = jnp.where(allowed, scores[:, span], masked_fill)
            prob = jnp.exp(masked - stats[0:1, :])
            probs.append(prob.astype(low))
            dscores.append((prob * (dprob[:, span] + stats[1:2, :])).astype(low))
        grad_value = grad_value + dot_f32(jnp.concatenate(probs, axis=1), cotangent, 1, 0)
        grad_key = grad_key + dot_f32(jnp.concatenate(dscores, axis=1), queries, 1, 0)
    grad_key = grad_key * scale
    own_ref[:, :head], own_ref[:, head:] = grad_key[:rows], grad_value[:rows]
    other_ref[:, :head], other_ref[:, head:] = grad_key[rows:], grad_value[rows:]


def relayout_kernel(y_count, tokens_ref, out_ref):
    members, _, columns = out_ref.shape
    quarter = columns // (2 * y_count)
    core = lax.axis_index("core")
    for member in range(members):
        x_hi, z_lo = member // 2, member % 2
        for half in range(2):
            for y in range(y_count):
                start = ((x_hi * y_count + y) * 4 + z_lo * 2 + (core ^ half)) * quarter
                target = (half * y_count + y) * quarter
                out_ref[member, :, target : target + quarter] = tokens_ref[
                    :, pl.ds(pl.multiple_of(start, quarter), quarter)
                ]


def near_kernel(x_ref, weight_ref, out_ref):
    out_ref[...] = dot_f32(x_ref[...], weight_ref[...], 1, 0)


def far_kernel(x_ref, weight_ref, sum_ref, out_ref):
    out_ref[...] = (sum_ref[...] + dot_f32(x_ref[...], weight_ref[...], 1, 0)).astype(low)


def split_kernel(parts_ref, q_ref, kv_ref, kv_copies, q_copies):
    head = q_ref.shape[1]
    total = parts_ref[0].astype(jnp.float32)
    for part in range(1, parts_ref.shape[0]):
        total = total + parts_ref[part].astype(jnp.float32)
    qkv = total.astype(low)
    queries, pairs = qkv[:, :head], qkv[:, head:]
    q_ref[...] = queries
    kv_ref[...] = pairs
    for copy in range(kv_copies.shape[0]):
        kv_copies[copy] = pairs
        q_copies[copy] = queries


def join_kernel(dq_ref, own_ref, other_ref, out_ref):
    pairs = (own_ref[...] + other_ref[...]).astype(low)
    rows = jnp.concatenate([dq_ref[...], pairs], axis=1)
    for copy in range(out_ref.shape[0]):
        out_ref[copy] = rows


def weight_kernel(x_ref, grad_ref, out_ref):
    out_ref[...] = dot_f32(x_ref[...], grad_ref[...], 0, 0).astype(out_ref.dtype)


def in_vmem(count):
    return [pl.BlockSpec(memory_space=pltpu.VMEM)] * count


def on_device(tokens, qkv_weight, out_grad):
    y_count, z_count = lax.axis_size("y"), lax.axis_size(z_axes)
    ctx_count = z_count * 4
    row_count, model, width = tokens.shape[1], tokens.shape[2], qkv_weight.shape[1]
    shard, head = qkv_weight.shape[0], qkv_weight.shape[1] // 3
    quarter, depth, group_rows = shard // 4, model // 8, 4 * row_count
    cotangent = out_grad[0]

    at = (lax.axis_index("zl") * 2 + lax.axis_index("core")) * quarter
    own_weight = lax.dynamic_slice_in_dim(qkv_weight, at, quarter)
    near = lax.all_gather(own_weight, "y", axis=0, tiled=True)
    far = swap(near, "core")
    split = pl.pallas_call(
        functools.partial(relayout_kernel, y_count),
        in_specs=in_vmem(1),
        out_specs=in_vmem(1)[0],
        out_shape=jax.ShapeDtypeStruct((4, row_count, 2 * depth), low),
        compiler_params=vmem,
        name="token_columns",
    )(tokens[0])
    columns = exchange(split, group_axes).reshape(group_rows, 2 * depth)
    whole = pl.BlockSpec((depth, width), lambda i: (0, 0))
    summed_rows = pl.BlockSpec((group_rows, width), lambda i: (0, 0))

    def column_half(half):
        return pl.BlockSpec((group_rows, depth), lambda i: (0, half))

    near_sum = pl.pallas_call(
        near_kernel,
        grid=(1,),
        in_specs=[column_half(0), whole],
        out_specs=summed_rows,
        out_shape=jax.ShapeDtypeStruct((group_rows, width), jnp.float32),
        compiler_params=vmem,
        name="near_projection",
    )(columns, near)
    parts = pl.pallas_call(
        far_kernel,
        grid=(1,),
        in_specs=[column_half(1), whole, summed_rows],
        out_specs=summed_rows,
        out_shape=jax.ShapeDtypeStruct((group_rows, width), low),
        compiler_params=vmem,
        name="far_projection",
    )(columns, far, near_sum)
    parts = exchange(parts.reshape(4, row_count, width), group_axes)
    cotangent_z = lax.all_gather(
        jnp.concatenate([cotangent] * 4, axis=1), z_axes, axis=0, tiled=True
    )
    parts, cotangent_z = lax.optimization_barrier((parts, cotangent_z))
    cotangent_z = cotangent_z[:, :head]
    cotangent_x = swap(cotangent_z, "xl")
    queries, own_pairs, pair_copies, query_copies = pl.pallas_call(
        split_kernel,
        in_specs=in_vmem(1),
        out_specs=in_vmem(4),
        out_shape=[
            jax.ShapeDtypeStruct(shape, low)
            for shape in (
                (row_count, head),
                (row_count, 2 * head),
                (z_count, row_count, 2 * head),
                (z_count, row_count, head),
            )
        ],
        compiler_params=vmem,
        name="projection_sum",
    )(parts)

    along_z = exchange(pair_copies, z_axes).reshape(-1, 2 * head)
    along_z, cotangent_x = lax.optimization_barrier((along_z, cotangent_x))
    by_x, by_core = swap(along_z, "xl"), swap(along_z, "core")
    pair_pieces = (along_z, by_x, by_core, swap(by_x, "core"))
    queries_z = exchange(query_copies, z_axes).reshape(-1, head)
    query_pieces = (queries_z, swap(queries_z, "xl"))

    attn_rows, stats, stat_columns = pl.pallas_call(
        functools.partial(forward_kernel, z_count),
        in_specs=in_vmem(6),
        out_specs=in_vmem(3),
        out_shape=[
            jax.ShapeDtypeStruct((row_count, head), low),
            jax.ShapeDtypeStruct((2 * z_count, 2, row_count), jnp.float32),
            jax.ShapeDtypeStruct((2, row_count, row_count), jnp.float32),
        ],
        scratch_shapes=[pltpu.VMEM((4, row_count, z_count * row_count), jnp.float32)],
        compiler_params=vmem,
        name="attention_rows",
    )(queries, *pair_pieces, cotangent)
    stats_all = exchange(stats, z_axes + ("xl",))
    grad_query = pl.pallas_call(
        functools.partial(query_kernel, z_count),
        in_specs=in_vmem(7),
        out_specs=in_vmem(1)[0],
        out_shape=jax.ShapeDtypeStruct((row_count, head), low),
        compiler_params=vmem,
        name="query_gradient",
    )(queries, *pair_pieces, cotangent, stat_columns)
    grad_query, stats_all = lax.optimization_barrier((grad_query, stats_all))

    own_part, other_part = pl.pallas_call(
        functools.partial(backward_kernel, z_count),
        in_specs=in_vmem(7),
        out_specs=in_vmem(2),
        out_shape=[jax.ShapeDtypeStruct((row_count, 2 * head), jnp.float32)] * 2,
        compiler_params=vmem,
        name="attention_columns",
    )(own_pairs, pair_pieces[2], *query_pieces, cotangent_z, cotangent_x, stats_all)
    grad_copies = pl.pallas_call(
        join_kernel,
        in_specs=in_vmem(3),
        out_specs=in_vmem(1)[0],
        out_shape=jax.ShapeDtypeStruct((4, row_count, width), low),
        compiler_params=vmem,
        name="join_gradients",
    )(grad_query, own_part, swap(other_part, "core"))
    grad_all = exchange(grad_copies, group_axes).reshape(group_rows, width)

    def weight_half(half, dtype):
        return pl.pallas_call(
            weight_kernel,
            grid=(1,),
            in_specs=[
                pl.BlockSpec((group_rows, depth), lambda i: (0, half)),
                pl.BlockSpec((group_rows, width), lambda i: (0, 0)),
            ],
            out_specs=pl.BlockSpec((depth, width), lambda i: (0, 0)),
            out_shape=jax.ShapeDtypeStruct((depth, width), dtype),
            compiler_params=vmem,
            name="weight_gradient",
        )(columns, grad_all)

    sent = swap(weight_half(1, low), "core")
    summed = (weight_half(0, jnp.float32) + sent.astype(jnp.float32)).astype(low)
    pieces = exchange(summed.reshape(z_count * y_count, -1, width), ("y", "zh", "xl"))
    own_piece = jnp.sum(pieces.astype(jnp.float32), axis=0).astype(low)
    on_core = spread(own_piece, z_axes + ("xl",), 2 * z_count)
    on_core = on_core.reshape((z_count // 2, 2, 2) + own_piece.shape).transpose(1, 0, 2, 3, 4)
    across = swap(on_core, "core")
    first = lax.axis_index("core") == 0
    total = jnp.stack([jnp.where(first, on_core, across), jnp.where(first, across, on_core)], axis=1)
    return (attn_rows[None], total.reshape(shard, width))


def solution(mesh):
    grid = Mesh(mesh.devices.reshape(2, 8, 4, 2, 2, 2), ("xh", "y") + ctx_axes)
    rows, weights = P(("xh", "y"), ctx_axes, None), P(("xh", "y"), None)
    return jax.shard_map(
        on_device,
        mesh=grid,
        in_specs=(rows, weights, rows),
        out_specs=(rows, weights),
        check_vma=False,
    )
```

```python
import functools
import math

import jax
import jax.numpy as jnp
from jax import lax
from jax.experimental import pallas as pl
from jax.experimental.pallas import tpu as pltpu
from jax.sharding import Mesh, PartitionSpec as P

z_weight = 0.001
masked_fill = -1e30
low = jnp.bfloat16
z_axes = ("zh", "zl")
ctx_axes = z_axes + ("xl", "core")
group_axes = ("xh", "zl")
vmem = pltpu.CompilerParams(vmem_limit_bytes=32 * 1024 * 1024)


def dot_f32(left, right, left_dim, right_dim):
    return lax.dot_general(
        left, right, (((left_dim,), (right_dim,)), ((), ())), preferred_element_type=jnp.float32
    )


def exchange(blocks, axes):
    return lax.all_to_all(blocks, axes, split_axis=0, concat_axis=0, tiled=True)


def spread(block, axes, count):
    return exchange(jnp.broadcast_to(block[None], (count,) + block.shape), axes)


def swap(block, axis):
    return lax.ppermute(block, axis, ((0, 1), (1, 0)))


def positions(device, inside, half_rows, ctx_count):
    block = jnp.where(inside < half_rows, device, 2 * ctx_count - 1 - device)
    return block * half_rows + inside % half_rows


def piece_device(piece, z):
    return z * 4 + (lax.axis_index("xl") ^ (piece & 1)) * 2 + (lax.axis_index("core") ^ (piece >> 1))


def forward_kernel(
    z_count, q_ref, kv0, kv1, kv2, kv3, cot_ref, attn_ref, stats_ref, dq_ref, held
):
    pieces = (kv0, kv1, kv2, kv3)
    rows, head = q_ref.shape
    half_rows, ctx_count = rows // 2, 4 * z_count
    scale = 1.0 / math.sqrt(head)
    own = piece_device(0, lax.axis_index(z_axes))
    down = lax.broadcasted_iota(jnp.int32, (rows, rows), 0)
    across = lax.broadcasted_iota(jnp.int32, (rows, rows), 1)
    own_positions = positions(own, down, half_rows, ctx_count)
    queries, cotangent = q_ref[...], cot_ref[...]
    top = None
    for piece, kv in enumerate(pieces):
        raw = dot_f32(queries, kv[:, :head], 1, 1) * scale
        for z in range(z_count):
            device = piece_device(piece, z)
            allowed = positions(device, across, half_rows, ctx_count) <= own_positions
            tile = jnp.where(allowed, raw[:, z * rows : (z + 1) * rows], masked_fill)
            held[piece, :, z * rows : (z + 1) * rows] = tile
            top = tile if top is None else jnp.maximum(top, tile)
    row_top = jnp.max(top, axis=1, keepdims=True)
    total = jnp.zeros((rows, rows), jnp.float32)
    for piece in range(4):
        weights = jnp.exp(held[piece] - row_top)
        held[piece] = weights
        for z in range(z_count):
            total = total + weights[:, z * rows : (z + 1) * rows]
    row_sum = jnp.sum(total, axis=1, keepdims=True)
    inverse = 1.0 / row_sum
    log_total = row_top + jnp.log(row_sum)
    attn = jnp.zeros((rows, head), jnp.float32)
    for piece, kv in enumerate(pieces):
        attn = attn + dot_f32((held[piece] * inverse).astype(low), kv[:, head:], 1, 0)
    attn_low = attn.astype(low)
    attn_ref[...] = attn_low
    delta = jnp.sum(
        cotangent.astype(jnp.float32) * attn_low.astype(jnp.float32), axis=1, keepdims=True
    )
    shift = 2.0 * z_weight * log_total - delta
    for place, column in enumerate((log_total, shift)):
        line = jnp.transpose(jnp.broadcast_to(column, (rows, rows)))[0:1, :]
        for copy in range(stats_ref.shape[0]):
            stats_ref[copy, place : place + 1, :] = line
    grad = jnp.zeros((rows, head), jnp.float32)
    for piece, kv in enumerate(pieces):
        dprob = dot_f32(cotangent, kv[:, head:], 1, 1)
        dscore = held[piece] * inverse * (dprob + shift)
        grad = grad + dot_f32(dscore.astype(low), kv[:, :head], 1, 0)
    dq_ref[...] = (grad * scale).astype(low)


def backward_kernel(z_count, along_ref, across_ref, qc0, qc1, stats_ref, own_ref, other_ref):
    rows, head = along_ref.shape[0] // z_count, along_ref.shape[1] // 2
    half_rows, ctx_count = rows // 2, 4 * z_count
    scale = 1.0 / math.sqrt(head)
    z_own = lax.axis_index(z_axes)
    down = lax.broadcasted_iota(jnp.int32, (rows, rows), 0)
    across = lax.broadcasted_iota(jnp.int32, (rows, rows), 1)
    key_positions = jnp.concatenate(
        [
            positions(piece_device(0, z_own), down, half_rows, ctx_count),
            positions(piece_device(2, z_own), down, half_rows, ctx_count),
        ],
        axis=0,
    )
    place = pl.ds(pl.multiple_of(z_own * rows, rows), rows)
    pairs = jnp.concatenate([along_ref[place, :], across_ref[place, :]], axis=0)
    keys, values = pairs[:, :head], pairs[:, head:]
    grad_key = jnp.zeros((2 * rows, head), jnp.float32)
    grad_value = jnp.zeros((2 * rows, head), jnp.float32)
    for piece, both in enumerate((qc0, qc1)):
        slot = lax.axis_index("xl") ^ piece
        queries, cotangent = both[:, :head], both[:, head:]
        scores = dot_f32(keys, queries, 1, 1) * scale
        dprob = dot_f32(values, cotangent, 1, 1)
        probs, dscores = [], []
        for z in range(z_count):
            span = slice(z * rows, (z + 1) * rows)
            stats = stats_ref[2 * z + slot]
            row_positions = positions(piece_device(piece, z), across, half_rows, ctx_count)
            allowed = key_positions <= jnp.concatenate([row_positions, row_positions], axis=0)
            masked = jnp.where(allowed, scores[:, span], masked_fill)
            prob = jnp.exp(masked - stats[0:1, :])
            probs.append(prob.astype(low))
            dscores.append((prob * (dprob[:, span] + stats[1:2, :])).astype(low))
        grad_value = grad_value + dot_f32(jnp.concatenate(probs, axis=1), cotangent, 1, 0)
        grad_key = grad_key + dot_f32(jnp.concatenate(dscores, axis=1), queries, 1, 0)
    grad_key = grad_key * scale
    own_ref[:, :head], own_ref[:, head:] = grad_key[:rows], grad_value[:rows]
    other_ref[:, :head], other_ref[:, head:] = grad_key[rows:], grad_value[rows:]


def relayout_kernel(y_count, tokens_ref, out_ref):
    members, _, columns = out_ref.shape
    quarter = columns // (2 * y_count)
    core = lax.axis_index("core")
    for member in range(members):
        x_hi, z_lo = member // 2, member % 2
        for half in range(2):
            for y in range(y_count):
                start = ((x_hi * y_count + y) * 4 + z_lo * 2 + (core ^ half)) * quarter
                target = (half * y_count + y) * quarter
                out_ref[member, :, target : target + quarter] = tokens_ref[
                    :, pl.ds(pl.multiple_of(start, quarter), quarter)
                ]


def near_kernel(x_ref, weight_ref, out_ref):
    out_ref[...] = dot_f32(x_ref[...], weight_ref[...], 1, 0)


def far_kernel(x_ref, weight_ref, sum_ref, out_ref):
    out_ref[...] = (sum_ref[...] + dot_f32(x_ref[...], weight_ref[...], 1, 0)).astype(low)


def split_kernel(parts_ref, cot_ref, q_ref, kv_copies, qc_copies):
    head = q_ref.shape[1]
    total = parts_ref[0].astype(jnp.float32)
    for part in range(1, parts_ref.shape[0]):
        total = total + parts_ref[part].astype(jnp.float32)
    qkv = total.astype(low)
    queries, pairs = qkv[:, :head], qkv[:, head:]
    q_ref[...] = queries
    both = jnp.concatenate([queries, cot_ref[...]], axis=1)
    for copy in range(kv_copies.shape[0]):
        kv_copies[copy] = pairs
        qc_copies[copy] = both


def join_kernel(dq_ref, own_ref, other_ref, out_ref):
    pairs = (own_ref[...] + other_ref[...]).astype(low)
    rows = jnp.concatenate([dq_ref[...], pairs], axis=1)
    for copy in range(out_ref.shape[0]):
        out_ref[copy] = rows


def weight_kernel(x_ref, grad_ref, out_ref):
    out_ref[...] = dot_f32(x_ref[...], grad_ref[...], 0, 0).astype(out_ref.dtype)


def in_vmem(count):
    return [pl.BlockSpec(memory_space=pltpu.VMEM)] * count


def on_device(tokens, qkv_weight, out_grad):
    y_count, z_count = lax.axis_size("y"), lax.axis_size(z_axes)
    ctx_count = z_count * 4
    row_count, model, width = tokens.shape[1], tokens.shape[2], qkv_weight.shape[1]
    shard, head = qkv_weight.shape[0], qkv_weight.shape[1] // 3
    quarter, depth, group_rows = shard // 4, model // 8, 4 * row_count
    cotangent = out_grad[0]

    at = (lax.axis_index("zl") * 2 + lax.axis_index("core")) * quarter
    own_weight = lax.dynamic_slice_in_dim(qkv_weight, at, quarter)
    near = lax.all_gather(own_weight, "y", axis=0, tiled=True)
    far = swap(near, "core")
    split = pl.pallas_call(
        functools.partial(relayout_kernel, y_count),
        in_specs=in_vmem(1),
        out_specs=in_vmem(1)[0],
        out_shape=jax.ShapeDtypeStruct((4, row_count, 2 * depth), low),
        compiler_params=vmem,
        name="token_columns",
    )(tokens[0])
    columns = exchange(split, group_axes).reshape(group_rows, 2 * depth)
    whole = pl.BlockSpec((depth, width), lambda i: (0, 0))
    summed_rows = pl.BlockSpec((group_rows, width), lambda i: (0, 0))

    def column_half(half):
        return pl.BlockSpec((group_rows, depth), lambda i: (0, half))

    near_sum = pl.pallas_call(
        near_kernel,
        grid=(1,),
        in_specs=[column_half(0), whole],
        out_specs=summed_rows,
        out_shape=jax.ShapeDtypeStruct((group_rows, width), jnp.float32),
        compiler_params=vmem,
        name="near_projection",
    )(columns, near)
    parts = pl.pallas_call(
        far_kernel,
        grid=(1,),
        in_specs=[column_half(1), whole, summed_rows],
        out_specs=summed_rows,
        out_shape=jax.ShapeDtypeStruct((group_rows, width), low),
        compiler_params=vmem,
        name="far_projection",
    )(columns, far, near_sum)
    parts = exchange(parts.reshape(4, row_count, width), group_axes)
    queries, pair_copies, query_copies = pl.pallas_call(
        split_kernel,
        in_specs=in_vmem(2),
        out_specs=in_vmem(3),
        out_shape=[
            jax.ShapeDtypeStruct(shape, low)
            for shape in (
                (row_count, head),
                (z_count, row_count, 2 * head),
                (z_count, row_count, 2 * head),
            )
        ],
        compiler_params=vmem,
        name="projection_sum",
    )(parts, cotangent)

    along_z = exchange(pair_copies, z_axes).reshape(-1, 2 * head)
    by_x, by_core = swap(along_z, "xl"), swap(along_z, "core")
    pair_pieces = (along_z, by_x, by_core, swap(by_x, "core"))
    queries_z = exchange(query_copies, z_axes).reshape(-1, 2 * head)
    query_pieces = (queries_z, swap(queries_z, "xl"))

    attn_rows, stats, grad_query = pl.pallas_call(
        functools.partial(forward_kernel, z_count),
        in_specs=in_vmem(6),
        out_specs=in_vmem(3),
        out_shape=[
            jax.ShapeDtypeStruct((row_count, head), low),
            jax.ShapeDtypeStruct((2 * z_count, 2, row_count), jnp.float32),
            jax.ShapeDtypeStruct((row_count, head), low),
        ],
        scratch_shapes=[pltpu.VMEM((4, row_count, z_count * row_count), jnp.float32)],
        compiler_params=vmem,
        name="attention_rows",
    )(queries, *pair_pieces, cotangent)
    stats_all = exchange(stats, z_axes + ("xl",))

    own_part, other_part = pl.pallas_call(
        functools.partial(backward_kernel, z_count),
        in_specs=in_vmem(5),
        out_specs=in_vmem(2),
        out_shape=[jax.ShapeDtypeStruct((row_count, 2 * head), jnp.float32)] * 2,
        compiler_params=vmem,
        name="attention_columns",
    )(pair_pieces[0], pair_pieces[2], *query_pieces, stats_all)
    grad_copies = pl.pallas_call(
        join_kernel,
        in_specs=in_vmem(3),
        out_specs=in_vmem(1)[0],
        out_shape=jax.ShapeDtypeStruct((4, row_count, width), low),
        compiler_params=vmem,
        name="join_gradients",
    )(grad_query, own_part, swap(other_part, "core"))
    grad_all = exchange(grad_copies, group_axes).reshape(group_rows, width)

    def weight_half(half, dtype):
        return pl.pallas_call(
            weight_kernel,
            grid=(1,),
            in_specs=[
                pl.BlockSpec((group_rows, depth), lambda i: (0, half)),
                pl.BlockSpec((group_rows, width), lambda i: (0, 0)),
            ],
            out_specs=pl.BlockSpec((depth, width), lambda i: (0, 0)),
            out_shape=jax.ShapeDtypeStruct((depth, width), dtype),
            compiler_params=vmem,
            name="weight_gradient",
        )(columns, grad_all)

    sent = swap(weight_half(1, low), "core")
    summed = (weight_half(0, jnp.float32) + sent.astype(jnp.float32)).astype(low)
    pieces = exchange(summed.reshape(z_count * y_count, -1, width), ("y", "zh", "xl"))
    own_piece = jnp.sum(pieces.astype(jnp.float32), axis=0).astype(low)
    on_core = spread(own_piece, z_axes + ("xl",), 2 * z_count)
    on_core = on_core.reshape((z_count // 2, 2, 2) + own_piece.shape).transpose(1, 0, 2, 3, 4)
    across = swap(on_core, "core")
    first = lax.axis_index("core") == 0
    total = jnp.stack([jnp.where(first, on_core, across), jnp.where(first, across, on_core)], axis=1)
    return (attn_rows[None], total.reshape(shard, width))


def solution(mesh):
    grid = Mesh(mesh.devices.reshape(2, 8, 4, 2, 2, 2), ("xh", "y") + ctx_axes)
    rows, weights = P(("xh", "y"), ctx_axes, None), P(("xh", "y"), None)
    return jax.shard_map(
        on_device,
        mesh=grid,
        in_specs=(rows, weights, rows),
        out_specs=(rows, weights),
        check_vma=False,
    )
```

```python
import functools
import math

import jax
import jax.numpy as jnp
from jax import lax
from jax.experimental import pallas as pl
from jax.experimental.pallas import tpu as pltpu
from jax.sharding import Mesh, PartitionSpec as P

z_weight = 0.001
masked_fill = -1e30
low = jnp.bfloat16
z_axes = ("zh", "zl")
ctx_axes = z_axes + ("xl", "core")
group_axes = ("xh", "zl")
vmem = pltpu.CompilerParams(vmem_limit_bytes=32 * 1024 * 1024)


def dot_f32(left, right, left_dim, right_dim):
    return lax.dot_general(
        left, right, (((left_dim,), (right_dim,)), ((), ())), preferred_element_type=jnp.float32
    )


def exchange(blocks, axes):
    return lax.all_to_all(blocks, axes, split_axis=0, concat_axis=0, tiled=True)


def spread(block, axes, count):
    return exchange(jnp.broadcast_to(block[None], (count,) + block.shape), axes)


def swap(block, axis):
    return lax.ppermute(block, axis, ((0, 1), (1, 0)))


def positions(device, inside, half_rows, ctx_count):
    block = jnp.where(inside < half_rows, device, 2 * ctx_count - 1 - device)
    return block * half_rows + inside % half_rows


def piece_device(piece, z):
    return z * 4 + (lax.axis_index("xl") ^ (piece & 1)) * 2 + (lax.axis_index("core") ^ (piece >> 1))


def forward_kernel(
    z_count, rows_ref, kv0, kv1, kv2, kv3, attn_ref, stats_ref, dq_ref, held
):
    pieces = (kv0, kv1, kv2, kv3)
    rows, head = attn_ref.shape
    half_rows, ctx_count = rows // 2, 4 * z_count
    scale = 1.0 / math.sqrt(head)
    own = piece_device(0, lax.axis_index(z_axes))
    down = lax.broadcasted_iota(jnp.int32, (rows, rows), 0)
    across = lax.broadcasted_iota(jnp.int32, (rows, rows), 1)
    own_positions = positions(own, down, half_rows, ctx_count)
    queries, cotangent = rows_ref[:, :head], rows_ref[:, head:]
    top = None
    for piece, kv in enumerate(pieces):
        raw = dot_f32(queries, kv[:, :head], 1, 1) * scale
        for z in range(z_count):
            device = piece_device(piece, z)
            allowed = positions(device, across, half_rows, ctx_count) <= own_positions
            tile = jnp.where(allowed, raw[:, z * rows : (z + 1) * rows], masked_fill)
            held[piece, :, z * rows : (z + 1) * rows] = tile
            top = tile if top is None else jnp.maximum(top, tile)
    row_top = jnp.max(top, axis=1, keepdims=True)
    total = jnp.zeros((rows, rows), jnp.float32)
    for piece in range(4):
        weights = jnp.exp(held[piece] - row_top)
        held[piece] = weights
        for z in range(z_count):
            total = total + weights[:, z * rows : (z + 1) * rows]
    row_sum = jnp.sum(total, axis=1, keepdims=True)
    inverse = 1.0 / row_sum
    log_total = row_top + jnp.log(row_sum)
    attn = jnp.zeros((rows, head), jnp.float32)
    for piece, kv in enumerate(pieces):
        attn = attn + dot_f32((held[piece] * inverse).astype(low), kv[:, head:], 1, 0)
    attn_low = attn.astype(low)
    attn_ref[...] = attn_low
    delta = jnp.sum(
        cotangent.astype(jnp.float32) * attn_low.astype(jnp.float32), axis=1, keepdims=True
    )
    shift = 2.0 * z_weight * log_total - delta
    for place, column in enumerate((log_total, shift)):
        line = jnp.transpose(jnp.broadcast_to(column, (rows, rows)))[0:1, :]
        for copy in range(stats_ref.shape[0]):
            stats_ref[copy, place : place + 1, :] = line
    grad = jnp.zeros((rows, head), jnp.float32)
    for piece, kv in enumerate(pieces):
        dprob = dot_f32(cotangent, kv[:, head:], 1, 1)
        dscore = held[piece] * inverse * (dprob + shift)
        grad = grad + dot_f32(dscore.astype(low), kv[:, :head], 1, 0)
    dq_ref[...] = (grad * scale).astype(low)


def backward_kernel(z_count, along_ref, across_ref, qc0, qc1, stats_ref, own_ref, other_ref):
    rows, head = along_ref.shape[0] // z_count, along_ref.shape[1] // 2
    half_rows, ctx_count = rows // 2, 4 * z_count
    scale = 1.0 / math.sqrt(head)
    z_own = lax.axis_index(z_axes)
    down = lax.broadcasted_iota(jnp.int32, (rows, rows), 0)
    across = lax.broadcasted_iota(jnp.int32, (rows, rows), 1)
    key_positions = jnp.concatenate(
        [
            positions(piece_device(0, z_own), down, half_rows, ctx_count),
            positions(piece_device(2, z_own), down, half_rows, ctx_count),
        ],
        axis=0,
    )
    place = pl.ds(pl.multiple_of(z_own * rows, rows), rows)
    pairs = jnp.concatenate([along_ref[place, :], across_ref[place, :]], axis=0)
    keys, values = pairs[:, :head], pairs[:, head:]
    grad_key = jnp.zeros((2 * rows, head), jnp.float32)
    grad_value = jnp.zeros((2 * rows, head), jnp.float32)
    for piece, both in enumerate((qc0, qc1)):
        slot = lax.axis_index("xl") ^ piece
        queries, cotangent = both[:, :head], both[:, head:]
        scores = dot_f32(keys, queries, 1, 1) * scale
        dprob = dot_f32(values, cotangent, 1, 1)
        probs, dscores = [], []
        for z in range(z_count):
            span = slice(z * rows, (z + 1) * rows)
            stats = stats_ref[2 * z + slot]
            row_positions = positions(piece_device(piece, z), across, half_rows, ctx_count)
            allowed = key_positions <= jnp.concatenate([row_positions, row_positions], axis=0)
            masked = jnp.where(allowed, scores[:, span], masked_fill)
            prob = jnp.exp(masked - stats[0:1, :])
            probs.append(prob.astype(low))
            dscores.append((prob * (dprob[:, span] + stats[1:2, :])).astype(low))
        grad_value = grad_value + dot_f32(jnp.concatenate(probs, axis=1), cotangent, 1, 0)
        grad_key = grad_key + dot_f32(jnp.concatenate(dscores, axis=1), queries, 1, 0)
    grad_key = grad_key * scale
    own_ref[:, :head], own_ref[:, head:] = grad_key[:rows], grad_value[:rows]
    other_ref[:, :head], other_ref[:, head:] = grad_key[rows:], grad_value[rows:]


def relayout_kernel(y_count, tokens_ref, out_ref, taken, placed, in_sems, out_sems):
    members, rows, columns = out_ref.shape
    quarter = columns // (2 * y_count)
    core = lax.axis_index("core")
    steps = in_sems.shape[0]
    spans = [pl.ds(step * (rows // steps), rows // steps) for step in range(steps)]
    reads = [
        pltpu.make_async_copy(tokens_ref.at[span], taken.at[span], in_sems.at[step])
        for step, span in enumerate(spans)
    ]
    writes = [
        pltpu.make_async_copy(placed.at[:, span], out_ref.at[:, span], out_sems.at[step])
        for step, span in enumerate(spans)
    ]
    for read in reads:
        read.start()
    for span, read, write in zip(spans, reads, writes):
        read.wait()
        for member in range(members):
            x_hi, z_lo = member // 2, member % 2
            for half in range(2):
                for y in range(y_count):
                    start = ((x_hi * y_count + y) * 4 + z_lo * 2 + (core ^ half)) * quarter
                    target = (half * y_count + y) * quarter
                    placed[member, span, target : target + quarter] = taken[
                        span, pl.ds(pl.multiple_of(start, quarter), quarter)
                    ]
        write.start()
    for write in writes:
        write.wait()


def near_kernel(x_ref, weight_ref, out_ref):
    out_ref[...] = dot_f32(x_ref[...], weight_ref[...], 1, 0)


def far_kernel(x_ref, weight_ref, sum_ref, out_ref):
    out_ref[...] = (sum_ref[...] + dot_f32(x_ref[...], weight_ref[...], 1, 0)).astype(low)


def split_kernel(parts_ref, cot_ref, rows_ref, kv_copies, qc_copies):
    head = cot_ref.shape[1]
    total = parts_ref[0].astype(jnp.float32)
    for part in range(1, parts_ref.shape[0]):
        total = total + parts_ref[part].astype(jnp.float32)
    qkv = total.astype(low)
    queries, pairs = qkv[:, :head], qkv[:, head:]
    both = jnp.concatenate([queries, cot_ref[...]], axis=1)
    rows_ref[...] = both
    for copy in range(kv_copies.shape[0]):
        kv_copies[copy] = pairs
        qc_copies[copy] = both


def join_kernel(dq_ref, own_ref, other_ref, out_ref):
    pairs = (own_ref[...] + other_ref[...]).astype(low)
    rows = jnp.concatenate([dq_ref[...], pairs], axis=1)
    for copy in range(out_ref.shape[0]):
        out_ref[copy] = rows


def weight_kernel(x_ref, grad_ref, out_ref):
    out_ref[...] = dot_f32(x_ref[...], grad_ref[...], 0, 0).astype(out_ref.dtype)


def in_vmem(count):
    return [pl.BlockSpec(memory_space=pltpu.VMEM)] * count


def on_device(tokens, qkv_weight, out_grad):
    y_count, z_count = lax.axis_size("y"), lax.axis_size(z_axes)
    ctx_count = z_count * 4
    row_count, model, width = tokens.shape[1], tokens.shape[2], qkv_weight.shape[1]
    shard, head = qkv_weight.shape[0], qkv_weight.shape[1] // 3
    quarter, depth, group_rows = shard // 4, model // 8, 4 * row_count
    cotangent = out_grad[0]

    at = (lax.axis_index("zl") * 2 + lax.axis_index("core")) * quarter
    own_weight = lax.dynamic_slice_in_dim(qkv_weight, at, quarter)
    near = lax.all_gather(own_weight, "y", axis=0, tiled=True)
    far = swap(near, "core")
    split = pl.pallas_call(
        functools.partial(relayout_kernel, y_count),
        in_specs=[pl.BlockSpec(memory_space=pl.ANY)],
        out_specs=pl.BlockSpec(memory_space=pl.ANY),
        out_shape=jax.ShapeDtypeStruct((4, row_count, 2 * depth), low),
        scratch_shapes=[
            pltpu.VMEM((row_count, model), low),
            pltpu.VMEM((4, row_count, 2 * depth), low),
            pltpu.SemaphoreType.DMA((4,)),
            pltpu.SemaphoreType.DMA((4,)),
        ],
        compiler_params=vmem,
        name="token_columns",
    )(tokens[0])
    columns = exchange(split, group_axes).reshape(group_rows, 2 * depth)
    whole = pl.BlockSpec((depth, width), lambda i: (0, 0))
    summed_rows = pl.BlockSpec((group_rows, width), lambda i: (0, 0))

    def column_half(half):
        return pl.BlockSpec((group_rows, depth), lambda i: (0, half))

    near_sum = pl.pallas_call(
        near_kernel,
        grid=(1,),
        in_specs=[column_half(0), whole],
        out_specs=summed_rows,
        out_shape=jax.ShapeDtypeStruct((group_rows, width), jnp.float32),
        compiler_params=vmem,
        name="near_projection",
    )(columns, near)
    parts = pl.pallas_call(
        far_kernel,
        grid=(1,),
        in_specs=[column_half(1), whole, summed_rows],
        out_specs=summed_rows,
        out_shape=jax.ShapeDtypeStruct((group_rows, width), low),
        compiler_params=vmem,
        name="far_projection",
    )(columns, far, near_sum)
    parts = exchange(parts.reshape(4, row_count, width), group_axes)
    own_rows, pair_copies, query_copies = pl.pallas_call(
        split_kernel,
        in_specs=in_vmem(2),
        out_specs=in_vmem(3),
        out_shape=[
            jax.ShapeDtypeStruct(shape, low)
            for shape in (
                (row_count, 2 * head),
                (z_count, row_count, 2 * head),
                (z_count, row_count, 2 * head),
            )
        ],
        compiler_params=vmem,
        name="projection_sum",
    )(parts, cotangent)

    along_z = exchange(pair_copies, z_axes).reshape(-1, 2 * head)
    by_x, by_core = swap(along_z, "xl"), swap(along_z, "core")
    pair_pieces = (along_z, by_x, by_core, swap(by_x, "core"))
    queries_z = exchange(query_copies, z_axes).reshape(-1, 2 * head)

    attn_rows, stats, grad_query = pl.pallas_call(
        functools.partial(forward_kernel, z_count),
        in_specs=in_vmem(5),
        out_specs=in_vmem(3),
        out_shape=[
            jax.ShapeDtypeStruct((row_count, head), low),
            jax.ShapeDtypeStruct((2 * z_count, 2, row_count), jnp.float32),
            jax.ShapeDtypeStruct((row_count, head), low),
        ],
        scratch_shapes=[pltpu.VMEM((4, row_count, z_count * row_count), jnp.float32)],
        compiler_params=vmem,
        name="attention_rows",
    )(own_rows, *pair_pieces)
    queries_z, _ = lax.optimization_barrier((queries_z, stats))
    query_pieces = (queries_z, swap(queries_z, "xl"))
    stats_all = exchange(stats, z_axes + ("xl",))

    own_part, other_part = pl.pallas_call(
        functools.partial(backward_kernel, z_count),
        in_specs=in_vmem(5),
        out_specs=in_vmem(2),
        out_shape=[jax.ShapeDtypeStruct((row_count, 2 * head), jnp.float32)] * 2,
        compiler_params=vmem,
        name="attention_columns",
    )(pair_pieces[0], pair_pieces[2], *query_pieces, stats_all)
    grad_copies = pl.pallas_call(
        join_kernel,
        in_specs=in_vmem(3),
        out_specs=in_vmem(1)[0],
        out_shape=jax.ShapeDtypeStruct((4, row_count, width), low),
        compiler_params=vmem,
        name="join_gradients",
    )(grad_query, own_part, swap(other_part, "core"))
    grad_all = exchange(grad_copies, group_axes).reshape(group_rows, width)

    def weight_half(half, dtype):
        return pl.pallas_call(
            weight_kernel,
            grid=(1,),
            in_specs=[
                pl.BlockSpec((group_rows, depth), lambda i: (0, half)),
                pl.BlockSpec((group_rows, width), lambda i: (0, 0)),
            ],
            out_specs=pl.BlockSpec((depth, width), lambda i: (0, 0)),
            out_shape=jax.ShapeDtypeStruct((depth, width), dtype),
            compiler_params=vmem,
            name="weight_gradient",
        )(columns, grad_all)

    sent = swap(weight_half(1, low), "core")
    summed = (weight_half(0, jnp.float32) + sent.astype(jnp.float32)).astype(low)
    pieces = exchange(summed.reshape(z_count * y_count, -1, width), ("y", "zh", "xl"))
    own_piece = jnp.sum(pieces.astype(jnp.float32), axis=0).astype(low)
    on_core = spread(own_piece, z_axes + ("xl",), 2 * z_count)
    on_core = on_core.reshape((z_count // 2, 2, 2) + own_piece.shape).transpose(1, 0, 2, 3, 4)
    across = swap(on_core, "core")
    first = lax.axis_index("core") == 0
    total = jnp.stack([jnp.where(first, on_core, across), jnp.where(first, across, on_core)], axis=1)
    return (attn_rows[None], total.reshape(shard, width))


def solution(mesh):
    grid = Mesh(mesh.devices.reshape(2, 8, 4, 2, 2, 2), ("xh", "y") + ctx_axes)
    rows, weights = P(("xh", "y"), ctx_axes, None), P(("xh", "y"), None)
    return jax.shard_map(
        on_device,
        mesh=grid,
        in_specs=(rows, weights, rows),
        out_specs=(rows, weights),
        check_vma=False,
    )
```

```python
import functools
import math

import jax
import jax.numpy as jnp
from jax import lax
from jax.experimental import pallas as pl
from jax.experimental.pallas import tpu as pltpu
from jax.sharding import Mesh, PartitionSpec as P

z_weight = 0.001
masked_fill = -1e30
low = jnp.bfloat16
z_axes = ("zh", "zl")
ctx_axes = z_axes + ("xl", "core")
group_axes = ("xh", "zl")
vmem = pltpu.CompilerParams(vmem_limit_bytes=32 * 1024 * 1024)


def dot_f32(left, right, left_dim, right_dim):
    return lax.dot_general(
        left, right, (((left_dim,), (right_dim,)), ((), ())), preferred_element_type=jnp.float32
    )


def exchange(blocks, axes):
    return lax.all_to_all(blocks, axes, split_axis=0, concat_axis=0, tiled=True)


def spread(block, axes, count):
    return exchange(jnp.broadcast_to(block[None], (count,) + block.shape), axes)


def swap(block, axis):
    return lax.ppermute(block, axis, ((0, 1), (1, 0)))


def positions(device, inside, half_rows, ctx_count):
    block = jnp.where(inside < half_rows, device, 2 * ctx_count - 1 - device)
    return block * half_rows + inside % half_rows


def piece_device(piece, z):
    return z * 4 + (lax.axis_index("xl") ^ (piece & 1)) * 2 + (lax.axis_index("core") ^ (piece >> 1))


def forward_kernel(
    z_count, rows_ref, kv0, kv1, kv2, kv3, attn_ref, stats_ref, dq_ref, pairs_ref, held
):
    pieces = (kv0, kv1, kv2, kv3)
    rows, head = attn_ref.shape
    half_rows, ctx_count = rows // 2, 4 * z_count
    scale = 1.0 / math.sqrt(head)
    own = piece_device(0, lax.axis_index(z_axes))
    down = lax.broadcasted_iota(jnp.int32, (rows, rows), 0)
    across = lax.broadcasted_iota(jnp.int32, (rows, rows), 1)
    own_positions = positions(own, down, half_rows, ctx_count)
    place = pl.ds(pl.multiple_of(lax.axis_index(z_axes) * rows, rows), rows)
    pairs_ref[:rows, :], pairs_ref[rows:, :] = kv0[place, :], kv2[place, :]
    queries, cotangent = rows_ref[:, :head], rows_ref[:, head:]
    top = None
    for piece, kv in enumerate(pieces):
        raw = dot_f32(queries, kv[:, :head], 1, 1) * scale
        for z in range(z_count):
            device = piece_device(piece, z)
            allowed = positions(device, across, half_rows, ctx_count) <= own_positions
            tile = jnp.where(allowed, raw[:, z * rows : (z + 1) * rows], masked_fill)
            held[piece, :, z * rows : (z + 1) * rows] = tile
            top = tile if top is None else jnp.maximum(top, tile)
    row_top = jnp.max(top, axis=1, keepdims=True)
    total = jnp.zeros((rows, rows), jnp.float32)
    for piece in range(4):
        weights = jnp.exp(held[piece] - row_top)
        held[piece] = weights
        for z in range(z_count):
            total = total + weights[:, z * rows : (z + 1) * rows]
    row_sum = jnp.sum(total, axis=1, keepdims=True)
    inverse = 1.0 / row_sum
    log_total = row_top + jnp.log(row_sum)
    attn = jnp.zeros((rows, head), jnp.float32)
    for piece, kv in enumerate(pieces):
        attn = attn + dot_f32((held[piece] * inverse).astype(low), kv[:, head:], 1, 0)
    attn_low = attn.astype(low)
    attn_ref[...] = attn_low
    delta = jnp.sum(
        cotangent.astype(jnp.float32) * attn_low.astype(jnp.float32), axis=1, keepdims=True
    )
    shift = 2.0 * z_weight * log_total - delta
    for place, column in enumerate((log_total, shift)):
        line = jnp.transpose(jnp.broadcast_to(column, (rows, rows)))[0:1, :]
        for copy in range(stats_ref.shape[0]):
            stats_ref[copy, place : place + 1, :] = line
    grad = jnp.zeros((rows, head), jnp.float32)
    for piece, kv in enumerate(pieces):
        dprob = dot_f32(cotangent, kv[:, head:], 1, 1)
        dscore = held[piece] * inverse * (dprob + shift)
        grad = grad + dot_f32(dscore.astype(low), kv[:, :head], 1, 0)
    dq_ref[...] = (grad * scale).astype(low)


def backward_kernel(z_count, pairs_ref, qc0, qc1, stats_ref, own_ref, other_ref):
    rows, head = pairs_ref.shape[0] // 2, pairs_ref.shape[1] // 2
    half_rows, ctx_count = rows // 2, 4 * z_count
    scale = 1.0 / math.sqrt(head)
    z_own = lax.axis_index(z_axes)
    down = lax.broadcasted_iota(jnp.int32, (rows, rows), 0)
    across = lax.broadcasted_iota(jnp.int32, (rows, rows), 1)
    key_positions = jnp.concatenate(
        [
            positions(piece_device(0, z_own), down, half_rows, ctx_count),
            positions(piece_device(2, z_own), down, half_rows, ctx_count),
        ],
        axis=0,
    )
    keys, values = pairs_ref[:, :head], pairs_ref[:, head:]
    grad_key = jnp.zeros((2 * rows, head), jnp.float32)
    grad_value = jnp.zeros((2 * rows, head), jnp.float32)
    for piece, both in enumerate((qc0, qc1)):
        slot = lax.axis_index("xl") ^ piece
        queries, cotangent = both[:, :head], both[:, head:]
        scores = dot_f32(keys, queries, 1, 1) * scale
        dprob = dot_f32(values, cotangent, 1, 1)
        probs, dscores = [], []
        for z in range(z_count):
            span = slice(z * rows, (z + 1) * rows)
            stats = stats_ref[2 * z + slot]
            row_positions = positions(piece_device(piece, z), across, half_rows, ctx_count)
            allowed = key_positions <= jnp.concatenate([row_positions, row_positions], axis=0)
            masked = jnp.where(allowed, scores[:, span], masked_fill)
            prob = jnp.exp(masked - stats[0:1, :])
            probs.append(prob.astype(low))
            dscores.append((prob * (dprob[:, span] + stats[1:2, :])).astype(low))
        grad_value = grad_value + dot_f32(jnp.concatenate(probs, axis=1), cotangent, 1, 0)
        grad_key = grad_key + dot_f32(jnp.concatenate(dscores, axis=1), queries, 1, 0)
    grad_key = grad_key * scale
    own_ref[:, :head], own_ref[:, head:] = grad_key[:rows], grad_value[:rows]
    other_ref[:, :head], other_ref[:, head:] = grad_key[rows:], grad_value[rows:]


def relayout_kernel(y_count, tokens_ref, out_ref, taken, sems):
    members, rows, columns = out_ref.shape
    quarter = columns // (2 * y_count)
    core = lax.axis_index("core")
    steps = sems.shape[0]
    spans = [pl.ds(step * (rows // steps), rows // steps) for step in range(steps)]
    reads = [
        pltpu.make_async_copy(tokens_ref.at[span], taken.at[span], sems.at[step])
        for step, span in enumerate(spans)
    ]
    for read in reads:
        read.start()
    for span, read in zip(spans, reads):
        read.wait()
        for member in range(members):
            x_hi, z_lo = member // 2, member % 2
            for half in range(2):
                for y in range(y_count):
                    start = ((x_hi * y_count + y) * 4 + z_lo * 2 + (core ^ half)) * quarter
                    target = (half * y_count + y) * quarter
                    out_ref[member, span, target : target + quarter] = taken[
                        span, pl.ds(pl.multiple_of(start, quarter), quarter)
                    ]


def near_kernel(x_ref, weight_ref, out_ref):
    out_ref[...] = dot_f32(x_ref[...], weight_ref[...], 1, 0)


def far_kernel(x_ref, weight_ref, sum_ref, out_ref):
    out_ref[...] = (sum_ref[...] + dot_f32(x_ref[...], weight_ref[...], 1, 0)).astype(low)


def split_kernel(parts_ref, cot_ref, rows_ref, kv_copies, qc_copies):
    head = cot_ref.shape[1]
    total = parts_ref[0].astype(jnp.float32)
    for part in range(1, parts_ref.shape[0]):
        total = total + parts_ref[part].astype(jnp.float32)
    qkv = total.astype(low)
    queries, pairs = qkv[:, :head], qkv[:, head:]
    both = jnp.concatenate([queries, cot_ref[...]], axis=1)
    rows_ref[...] = both
    for copy in range(kv_copies.shape[0]):
        kv_copies[copy] = pairs
        qc_copies[copy] = both


def join_kernel(dq_ref, own_ref, other_ref, out_ref):
    pairs = (own_ref[...] + other_ref[...]).astype(low)
    rows = jnp.concatenate([dq_ref[...], pairs], axis=1)
    for copy in range(out_ref.shape[0]):
        out_ref[copy] = rows


def weight_kernel(x_ref, grad_ref, out_ref):
    out_ref[...] = dot_f32(x_ref[...], grad_ref[...], 0, 0).astype(out_ref.dtype)


def in_vmem(count):
    return [pl.BlockSpec(memory_space=pltpu.VMEM)] * count


def on_device(tokens, qkv_weight, out_grad):
    y_count, z_count = lax.axis_size("y"), lax.axis_size(z_axes)
    ctx_count = z_count * 4
    row_count, model, width = tokens.shape[1], tokens.shape[2], qkv_weight.shape[1]
    shard, head = qkv_weight.shape[0], qkv_weight.shape[1] // 3
    quarter, depth, group_rows = shard // 4, model // 8, 4 * row_count
    cotangent = out_grad[0]

    at = (lax.axis_index("zl") * 2 + lax.axis_index("core")) * quarter
    own_weight = lax.dynamic_slice_in_dim(qkv_weight, at, quarter)
    near = lax.all_gather(own_weight, "y", axis=0, tiled=True)
    far = swap(near, "core")
    split = pl.pallas_call(
        functools.partial(relayout_kernel, y_count),
        in_specs=[pl.BlockSpec(memory_space=pltpu.HBM)],
        out_specs=in_vmem(1)[0],
        out_shape=jax.ShapeDtypeStruct((4, row_count, 2 * depth), low),
        scratch_shapes=[
            pltpu.VMEM((row_count, model), low),
            pltpu.SemaphoreType.DMA((4,)),
        ],
        compiler_params=vmem,
        name="token_columns",
    )(pltpu.with_memory_space_constraint(tokens[0], pltpu.HBM))
    columns = exchange(split, group_axes).reshape(group_rows, 2 * depth)
    whole = pl.BlockSpec((depth, width), lambda i: (0, 0))
    summed_rows = pl.BlockSpec((group_rows, width), lambda i: (0, 0))

    def column_half(half):
        return pl.BlockSpec((group_rows, depth), lambda i: (0, half))

    near_sum = pl.pallas_call(
        near_kernel,
        grid=(1,),
        in_specs=[column_half(0), whole],
        out_specs=summed_rows,
        out_shape=jax.ShapeDtypeStruct((group_rows, width), jnp.float32),
        compiler_params=vmem,
        name="near_projection",
    )(columns, near)
    parts = pl.pallas_call(
        far_kernel,
        grid=(1,),
        in_specs=[column_half(1), whole, summed_rows],
        out_specs=summed_rows,
        out_shape=jax.ShapeDtypeStruct((group_rows, width), low),
        compiler_params=vmem,
        name="far_projection",
    )(columns, far, near_sum)
    parts = exchange(parts.reshape(4, row_count, width), group_axes)
    own_rows, pair_copies, query_copies = pl.pallas_call(
        split_kernel,
        in_specs=in_vmem(2),
        out_specs=in_vmem(3),
        out_shape=[
            jax.ShapeDtypeStruct(shape, low)
            for shape in (
                (row_count, 2 * head),
                (z_count, row_count, 2 * head),
                (z_count, row_count, 2 * head),
            )
        ],
        compiler_params=vmem,
        name="projection_sum",
    )(parts, cotangent)

    along_z = exchange(pair_copies, z_axes).reshape(-1, 2 * head)
    by_x, by_core = swap(along_z, "xl"), swap(along_z, "core")
    pair_pieces = (along_z, by_x, by_core, swap(by_x, "core"))
    queries_z = exchange(query_copies, z_axes).reshape(-1, 2 * head)

    attn_rows, stats, grad_query, both_pairs = pl.pallas_call(
        functools.partial(forward_kernel, z_count),
        in_specs=in_vmem(5),
        out_specs=in_vmem(4),
        out_shape=[
            jax.ShapeDtypeStruct((row_count, head), low),
            jax.ShapeDtypeStruct((2 * z_count, 2, row_count), jnp.float32),
            jax.ShapeDtypeStruct((row_count, head), low),
            jax.ShapeDtypeStruct((2 * row_count, 2 * head), low),
        ],
        scratch_shapes=[pltpu.VMEM((4, row_count, z_count * row_count), jnp.float32)],
        compiler_params=vmem,
        name="attention_rows",
    )(own_rows, *pair_pieces)
    queries_z, _ = lax.optimization_barrier((queries_z, stats))
    query_pieces = (queries_z, swap(queries_z, "xl"))
    stats_all = exchange(stats, z_axes + ("xl",))

    own_part, other_part = pl.pallas_call(
        functools.partial(backward_kernel, z_count),
        in_specs=in_vmem(4),
        out_specs=in_vmem(2),
        out_shape=[jax.ShapeDtypeStruct((row_count, 2 * head), jnp.float32)] * 2,
        compiler_params=vmem,
        name="attention_columns",
    )(both_pairs, *query_pieces, stats_all)
    grad_copies = pl.pallas_call(
        join_kernel,
        in_specs=in_vmem(3),
        out_specs=in_vmem(1)[0],
        out_shape=jax.ShapeDtypeStruct((4, row_count, width), low),
        compiler_params=vmem,
        name="join_gradients",
    )(grad_query, own_part, swap(other_part, "core"))
    grad_all = exchange(grad_copies, group_axes).reshape(group_rows, width)

    def weight_half(half, dtype):
        return pl.pallas_call(
            weight_kernel,
            grid=(1,),
            in_specs=[
                pl.BlockSpec((group_rows, depth), lambda i: (0, half)),
                pl.BlockSpec((group_rows, width), lambda i: (0, 0)),
            ],
            out_specs=pl.BlockSpec((depth, width), lambda i: (0, 0)),
            out_shape=jax.ShapeDtypeStruct((depth, width), dtype),
            compiler_params=vmem,
            name="weight_gradient",
        )(columns, grad_all)

    sent = swap(weight_half(1, low), "core")
    summed = (weight_half(0, jnp.float32) + sent.astype(jnp.float32)).astype(low)
    pieces = exchange(summed.reshape(z_count * y_count, -1, width), ("y", "zh", "xl"))
    own_piece = jnp.sum(pieces.astype(jnp.float32), axis=0).astype(low)
    on_core = spread(own_piece, z_axes + ("xl",), 2 * z_count)
    on_core = on_core.reshape((z_count // 2, 2, 2) + own_piece.shape).transpose(1, 0, 2, 3, 4)
    across = swap(on_core, "core")
    first = lax.axis_index("core") == 0
    total = jnp.stack([jnp.where(first, on_core, across), jnp.where(first, across, on_core)], axis=1)
    return (attn_rows[None], total.reshape(shard, width))


def solution(mesh):
    grid = Mesh(mesh.devices.reshape(2, 8, 4, 2, 2, 2), ("xh", "y") + ctx_axes)
    rows, weights = P(("xh", "y"), ctx_axes, None), P(("xh", "y"), None)
    return jax.shard_map(
        on_device,
        mesh=grid,
        in_specs=(rows, weights, rows),
        out_specs=(rows, weights),
        check_vma=False,
    )
```

```python
import functools
import math

import jax
import jax.numpy as jnp
from jax import lax
from jax.experimental import pallas as pl
from jax.experimental.pallas import tpu as pltpu
from jax.sharding import Mesh, PartitionSpec as P

z_weight = 0.001
masked_fill = -1e30
low = jnp.bfloat16
z_axes = ("zh", "zl")
ctx_axes = z_axes + ("xl", "core")
group_axes = ("xh", "zl")
vmem = pltpu.CompilerParams(vmem_limit_bytes=32 * 1024 * 1024)


def dot_f32(left, right, left_dim, right_dim):
    return lax.dot_general(
        left, right, (((left_dim,), (right_dim,)), ((), ())), preferred_element_type=jnp.float32
    )


def exchange(blocks, axes):
    return lax.all_to_all(blocks, axes, split_axis=0, concat_axis=0, tiled=True)


def spread(block, axes, count):
    return exchange(jnp.broadcast_to(block[None], (count,) + block.shape), axes)


def swap(block, axis):
    return lax.ppermute(block, axis, ((0, 1), (1, 0)))


def positions(device, inside, half_rows, ctx_count):
    block = jnp.where(inside < half_rows, device, 2 * ctx_count - 1 - device)
    return block * half_rows + inside % half_rows


def piece_device(piece, z):
    return z * 4 + (lax.axis_index("xl") ^ (piece & 1)) * 2 + (lax.axis_index("core") ^ (piece >> 1))


def forward_kernel(
    z_count, rows_ref, kv0, kv1, kv2, kv3, attn_ref, stats_ref, dq_ref, pairs_ref, held
):
    pieces = (kv0, kv1, kv2, kv3)
    rows, head = attn_ref.shape
    half_rows, ctx_count = rows // 2, 4 * z_count
    scale = 1.0 / math.sqrt(head)
    own = piece_device(0, lax.axis_index(z_axes))
    down = lax.broadcasted_iota(jnp.int32, (rows, rows), 0)
    across = lax.broadcasted_iota(jnp.int32, (rows, rows), 1)
    own_positions = positions(own, down, half_rows, ctx_count)
    place = pl.ds(pl.multiple_of(lax.axis_index(z_axes) * rows, rows), rows)
    pairs_ref[:rows, :], pairs_ref[rows:, :] = kv0[place, :], kv2[place, :]
    queries, cotangent = rows_ref[:, :head], rows_ref[:, head:]
    top = None
    for piece, kv in enumerate(pieces):
        raw = dot_f32(queries, kv[:, :head], 1, 1) * scale
        for z in range(z_count):
            device = piece_device(piece, z)
            allowed = positions(device, across, half_rows, ctx_count) <= own_positions
            tile = jnp.where(allowed, raw[:, z * rows : (z + 1) * rows], masked_fill)
            held[piece, :, z * rows : (z + 1) * rows] = tile
            top = tile if top is None else jnp.maximum(top, tile)
    row_top = jnp.max(top, axis=1, keepdims=True)
    total = jnp.zeros((rows, rows), jnp.float32)
    for piece in range(4):
        weights = jnp.exp(held[piece] - row_top)
        held[piece] = weights
        for z in range(z_count):
            total = total + weights[:, z * rows : (z + 1) * rows]
    row_sum = jnp.sum(total, axis=1, keepdims=True)
    inverse = 1.0 / row_sum
    log_total = row_top + jnp.log(row_sum)
    attn = jnp.zeros((rows, head), jnp.float32)
    for piece, kv in enumerate(pieces):
        attn = attn + dot_f32((held[piece] * inverse).astype(low), kv[:, head:], 1, 0)
    attn_low = attn.astype(low)
    attn_ref[...] = attn_low
    delta = jnp.sum(
        cotangent.astype(jnp.float32) * attn_low.astype(jnp.float32), axis=1, keepdims=True
    )
    shift = 2.0 * z_weight * log_total - delta
    for place, column in enumerate((log_total, shift)):
        line = jnp.transpose(jnp.broadcast_to(column, (rows, rows)))[0:1, :]
        for copy in range(stats_ref.shape[0]):
            stats_ref[copy, place : place + 1, :] = line
    grad = jnp.zeros((rows, head), jnp.float32)
    for piece, kv in enumerate(pieces):
        dprob = dot_f32(cotangent, kv[:, head:], 1, 1)
        dscore = held[piece] * inverse * (dprob + shift)
        grad = grad + dot_f32(dscore.astype(low), kv[:, :head], 1, 0)
    dq_ref[...] = (grad * scale).astype(low)


def backward_kernel(z_count, pairs_ref, qc0, qc1, stats_ref, own_ref, other_ref):
    rows, head = pairs_ref.shape[0] // 2, pairs_ref.shape[1] // 2
    half_rows, ctx_count = rows // 2, 4 * z_count
    scale = 1.0 / math.sqrt(head)
    z_own = lax.axis_index(z_axes)
    down = lax.broadcasted_iota(jnp.int32, (rows, rows), 0)
    across = lax.broadcasted_iota(jnp.int32, (rows, rows), 1)
    key_positions = jnp.concatenate(
        [
            positions(piece_device(0, z_own), down, half_rows, ctx_count),
            positions(piece_device(2, z_own), down, half_rows, ctx_count),
        ],
        axis=0,
    )
    keys, values = pairs_ref[:, :head], pairs_ref[:, head:]
    grad_key = jnp.zeros((2 * rows, head), jnp.float32)
    grad_value = jnp.zeros((2 * rows, head), jnp.float32)
    for piece, both in enumerate((qc0, qc1)):
        slot = lax.axis_index("xl") ^ piece
        queries, cotangent = both[:, :head], both[:, head:]
        scores = dot_f32(keys, queries, 1, 1) * scale
        dprob = dot_f32(values, cotangent, 1, 1)
        probs, dscores = [], []
        for z in range(z_count):
            span = slice(z * rows, (z + 1) * rows)
            stats = stats_ref[2 * z + slot]
            row_positions = positions(piece_device(piece, z), across, half_rows, ctx_count)
            allowed = key_positions <= jnp.concatenate([row_positions, row_positions], axis=0)
            masked = jnp.where(allowed, scores[:, span], masked_fill)
            prob = jnp.exp(masked - stats[0:1, :])
            probs.append(prob.astype(low))
            dscores.append((prob * (dprob[:, span] + stats[1:2, :])).astype(low))
        grad_value = grad_value + dot_f32(jnp.concatenate(probs, axis=1), cotangent, 1, 0)
        grad_key = grad_key + dot_f32(jnp.concatenate(dscores, axis=1), queries, 1, 0)
    grad_key = grad_key * scale
    own_ref[:, :head], own_ref[:, head:] = grad_key[:rows], grad_value[:rows]
    other_ref[:, :head], other_ref[:, head:] = grad_key[rows:], grad_value[rows:]


def relayout_kernel(y_count, tokens_ref, out_ref, taken, sems):
    members, rows, columns = out_ref.shape
    quarter = columns // (2 * y_count)
    core = lax.axis_index("core")
    steps = sems.shape[0]
    spans = [pl.ds(step * (rows // steps), rows // steps) for step in range(steps)]
    reads = [
        pltpu.make_async_copy(tokens_ref.at[span], taken.at[span], sems.at[step])
        for step, span in enumerate(spans)
    ]
    for read in reads:
        read.start()
    for span, read in zip(spans, reads):
        read.wait()
        for member in range(members):
            x_hi, z_lo = member // 2, member % 2
            for half in range(2):
                for y in range(y_count):
                    start = ((x_hi * y_count + y) * 4 + z_lo * 2 + (core ^ half)) * quarter
                    target = (half * y_count + y) * quarter
                    out_ref[member, span, target : target + quarter] = taken[
                        span, pl.ds(pl.multiple_of(start, quarter), quarter)
                    ]


def near_kernel(x_ref, weight_ref, out_ref):
    out_ref[...] = dot_f32(x_ref[...], weight_ref[...], 1, 0)


def far_kernel(x_ref, weight_ref, sum_ref, out_ref):
    out_ref[...] = (sum_ref[...] + dot_f32(x_ref[...], weight_ref[...], 1, 0)).astype(low)


def split_kernel(parts_ref, cot_ref, rows_ref, kv_copies, qc_copies):
    head = cot_ref.shape[1]
    total = parts_ref[0].astype(jnp.float32)
    for part in range(1, parts_ref.shape[0]):
        total = total + parts_ref[part].astype(jnp.float32)
    qkv = total.astype(low)
    queries, pairs = qkv[:, :head], qkv[:, head:]
    both = jnp.concatenate([queries, cot_ref[...]], axis=1)
    rows_ref[...] = both
    for copy in range(kv_copies.shape[0]):
        kv_copies[copy] = pairs
        qc_copies[copy] = both


def join_kernel(dq_ref, own_ref, other_ref, out_ref):
    pairs = (own_ref[...] + other_ref[...]).astype(low)
    out_ref[...] = jnp.concatenate([dq_ref[...], pairs], axis=1)


def weight_kernel(x_ref, grad_ref, out_ref):
    out_ref[...] = dot_f32(x_ref[...], grad_ref[...], 0, 0).astype(out_ref.dtype)


def in_vmem(count):
    return [pl.BlockSpec(memory_space=pltpu.VMEM)] * count


def on_device(tokens, qkv_weight, out_grad):
    y_count, z_count = lax.axis_size("y"), lax.axis_size(z_axes)
    ctx_count = z_count * 4
    row_count, model, width = tokens.shape[1], tokens.shape[2], qkv_weight.shape[1]
    shard, head = qkv_weight.shape[0], qkv_weight.shape[1] // 3
    quarter, depth, group_rows = shard // 4, model // 8, 4 * row_count
    cotangent = out_grad[0]

    at = (lax.axis_index("zl") * 2 + lax.axis_index("core")) * quarter
    own_weight = lax.dynamic_slice_in_dim(qkv_weight, at, quarter)
    near = lax.all_gather(own_weight, "y", axis=0, tiled=True)
    far = swap(near, "core")
    split = pl.pallas_call(
        functools.partial(relayout_kernel, y_count),
        in_specs=[pl.BlockSpec(memory_space=pltpu.HBM)],
        out_specs=in_vmem(1)[0],
        out_shape=jax.ShapeDtypeStruct((4, row_count, 2 * depth), low),
        scratch_shapes=[
            pltpu.VMEM((row_count, model), low),
            pltpu.SemaphoreType.DMA((4,)),
        ],
        compiler_params=vmem,
        name="token_columns",
    )(pltpu.with_memory_space_constraint(tokens[0], pltpu.HBM))
    columns = exchange(split, group_axes).reshape(group_rows, 2 * depth)
    whole = pl.BlockSpec((depth, width), lambda i: (0, 0))
    summed_rows = pl.BlockSpec((group_rows, width), lambda i: (0, 0))

    def column_half(half):
        return pl.BlockSpec((group_rows, depth), lambda i: (0, half))

    near_sum = pl.pallas_call(
        near_kernel,
        grid=(1,),
        in_specs=[column_half(0), whole],
        out_specs=summed_rows,
        out_shape=jax.ShapeDtypeStruct((group_rows, width), jnp.float32),
        compiler_params=vmem,
        name="near_projection",
    )(columns, near)
    parts = pl.pallas_call(
        far_kernel,
        grid=(1,),
        in_specs=[column_half(1), whole, summed_rows],
        out_specs=summed_rows,
        out_shape=jax.ShapeDtypeStruct((group_rows, width), low),
        compiler_params=vmem,
        name="far_projection",
    )(columns, far, near_sum)
    parts = exchange(parts.reshape(4, row_count, width), group_axes)
    own_rows, pair_copies, query_copies = pl.pallas_call(
        split_kernel,
        in_specs=in_vmem(2),
        out_specs=in_vmem(3),
        out_shape=[
            jax.ShapeDtypeStruct(shape, low)
            for shape in (
                (row_count, 2 * head),
                (z_count, row_count, 2 * head),
                (z_count, row_count, 2 * head),
            )
        ],
        compiler_params=vmem,
        name="projection_sum",
    )(parts, cotangent)

    along_z = exchange(pair_copies, z_axes).reshape(-1, 2 * head)
    by_x, by_core = swap(along_z, "xl"), swap(along_z, "core")
    pair_pieces = (along_z, by_x, by_core, swap(by_x, "core"))
    queries_z = exchange(query_copies, z_axes).reshape(-1, 2 * head)

    attn_rows, stats, grad_query, both_pairs = pl.pallas_call(
        functools.partial(forward_kernel, z_count),
        in_specs=in_vmem(5),
        out_specs=in_vmem(4),
        out_shape=[
            jax.ShapeDtypeStruct((row_count, head), low),
            jax.ShapeDtypeStruct((2 * z_count, 2, row_count), jnp.float32),
            jax.ShapeDtypeStruct((row_count, head), low),
            jax.ShapeDtypeStruct((2 * row_count, 2 * head), low),
        ],
        scratch_shapes=[pltpu.VMEM((4, row_count, z_count * row_count), jnp.float32)],
        compiler_params=vmem,
        name="attention_rows",
    )(own_rows, *pair_pieces)
    queries_z, _ = lax.optimization_barrier((queries_z, stats))
    query_pieces = (queries_z, swap(queries_z, "xl"))
    stats_all = exchange(stats, z_axes + ("xl",))

    own_part, other_part = pl.pallas_call(
        functools.partial(backward_kernel, z_count),
        in_specs=in_vmem(4),
        out_specs=in_vmem(2),
        out_shape=[jax.ShapeDtypeStruct((row_count, 2 * head), jnp.float32)] * 2,
        compiler_params=vmem,
        name="attention_columns",
    )(both_pairs, *query_pieces, stats_all)
    grad_rows = pl.pallas_call(
        join_kernel,
        in_specs=in_vmem(3),
        out_specs=in_vmem(1)[0],
        out_shape=jax.ShapeDtypeStruct((row_count, width), low),
        compiler_params=vmem,
        name="join_gradients",
    )(grad_query, own_part, swap(other_part, "core"))
    grad_all = lax.all_gather(grad_rows, group_axes, axis=0, tiled=True)

    def weight_half(half, dtype):
        return pl.pallas_call(
            weight_kernel,
            grid=(1,),
            in_specs=[
                pl.BlockSpec((group_rows, depth), lambda i: (0, half)),
                pl.BlockSpec((group_rows, width), lambda i: (0, 0)),
            ],
            out_specs=pl.BlockSpec((depth, width), lambda i: (0, 0)),
            out_shape=jax.ShapeDtypeStruct((depth, width), dtype),
            compiler_params=vmem,
            name="weight_gradient",
        )(columns, grad_all)

    sent = swap(weight_half(1, low), "core")
    summed = (weight_half(0, jnp.float32) + sent.astype(jnp.float32)).astype(low)
    pieces = exchange(summed.reshape(z_count * y_count, -1, width), ("y", "zh", "xl"))
    own_piece = jnp.sum(pieces.astype(jnp.float32), axis=0).astype(low)
    on_core = spread(own_piece, z_axes + ("xl",), 2 * z_count)
    on_core = on_core.reshape((z_count // 2, 2, 2) + own_piece.shape).transpose(1, 0, 2, 3, 4)
    across = swap(on_core, "core")
    first = lax.axis_index("core") == 0
    total = jnp.stack([jnp.where(first, on_core, across), jnp.where(first, across, on_core)], axis=1)
    return (attn_rows[None], total.reshape(shard, width))


def solution(mesh):
    grid = Mesh(mesh.devices.reshape(2, 8, 4, 2, 2, 2), ("xh", "y") + ctx_axes)
    rows, weights = P(("xh", "y"), ctx_axes, None), P(("xh", "y"), None)
    return jax.shard_map(
        on_device,
        mesh=grid,
        in_specs=(rows, weights, rows),
        out_specs=(rows, weights),
        check_vma=False,
    )
```
